128 devices in a mesh: dp: 16 (over x, y), tensor: 8 (over z, core).
Axes of the slice: x: 4, y: 4, z: 4, core: 2. Of those that a mesh axis runs over, the one named last changes fastest.
Arguments:
- hidden_rows: bfloat16 [256, 32, 8192], P('tensor', 'dp'), may hold values from -6 to 6
- norm_gain: float32 [8192], replicated, may hold values from 0.1 to 1.9
- w_query: bfloat16 [8192, 4096], P(None, 'tensor'), may hold values from -0.0625 to 0.0625
- w_key: bfloat16 [8192, 1024], P(None, 'tensor'), may hold values from -0.0625 to 0.0625
- w_value: bfloat16 [8192, 1024], P(None, 'tensor'), may hold values from -0.0625 to 0.0625
- w_out: bfloat16 [4096, 8192], P('tensor'), may hold values from -1.5 to 1.5
- cache_keys: bfloat16 [32, 2048, 1024], P('dp', None, 'tensor'), may hold values from -6 to 6
- cache_values: bfloat16 [32, 2048, 1024], P('dp', None, 'tensor'), may hold values from -6 to 6
- slot_of_request: int32 [32], replicated, may hold values from 0 to 31, as said below
- span_length: int32 [32], replicated, may hold values from 1 to 256, as said below
- prefix_length: int32 [32], replicated, may hold values from 1 to 2048, as said below
Outputs:
- attention_out: bfloat16 [256, 32, 8192], P('tensor', 'dp')
The draws below stay inside these ranges and needn't reach their ends.
Inputs may be any that keep to these rules, and one draw needn't show every extreme that they name: `slot_of_request`: a permutation of the slots 0 to 31; slot i lies on dp index i // 2, request r starts on dp index r // 2; there are 2 distinct numbers m, one of them 1, the same for every dp index, such that the 2 requests of dp index i have their slots on the dp indices i XOR m, one on each. `span_length`: some request uses all 256 new positions. `prefix_length`: some request has all 2048 cached positions.
All inputs are finite; a program needn't handle non-finite values.
Results may differ from the reference program's by a relative error of at most 0.019.
Values may be sent and summed in bfloat16 or wider, within the bound.
A program may use at most 128 MiB of HBM per device.

```python
import jax
import jax.numpy as jnp
from jax import lax

D = 8192
HEADS = 32
KVH = 8
HD = 128
R_DEV = 2
SPAN = 256
PREFIX = 2048
REQUESTS = 32


def draw_slot_of_request(key, part):
    device_count = REQUESTS // R_DEV
    keys = jax.random.split(jax.random.fold_in(key, 101), 3)
    shuffled = jax.random.permutation(keys[0], device_count).astype(jnp.int32)
    where_one = jnp.argmax(shuffled == 1).astype(jnp.int32)
    shuffled = shuffled.at[where_one].set(shuffled[0]).at[0].set(1)
    dp_masks = shuffled[:R_DEV]
    slot_shift = jax.random.randint(keys[1], (device_count,), 0, R_DEV)
    request_shift = jax.random.randint(keys[2], (device_count,), 0, R_DEV)
    source_rows = jnp.arange(device_count, dtype=jnp.int32)[:, None]
    column = jnp.arange(R_DEV, dtype=jnp.int32)[None, :]
    target = jnp.bitwise_xor(source_rows, dp_masks[column])
    local_slot = (column + slot_shift[target]) % R_DEV
    local_request = (column + request_shift[source_rows]) % R_DEV
    request_index = (source_rows * R_DEV + local_request).reshape(-1)
    slot_index = (target * R_DEV + local_slot).reshape(-1)
    return jnp.zeros((REQUESTS,), jnp.int32).at[request_index].set(slot_index.astype(jnp.int32))


def draw_span_length(key, part):
    first_key, second_key = jax.random.split(jax.random.fold_in(key, 202))
    drawn = jax.random.randint(first_key, (REQUESTS,), 1, SPAN + 1)
    full_request = jax.random.randint(second_key, (), 0, REQUESTS)
    return drawn.at[full_request].set(SPAN).astype(jnp.int32)


def draw_prefix_length(key, part):
    first_key, second_key = jax.random.split(jax.random.fold_in(key, 303))
    drawn = jax.random.randint(first_key, (REQUESTS,), 1, PREFIX + 1)
    full_request = jax.random.randint(second_key, (), 0, REQUESTS)
    return drawn.at[full_request].set(PREFIX).astype(jnp.int32)


def shard_levels(key, extent, shards, low, largest):
    factor_of, own = 1.0, jax.random.fold_in(key, 6)
    for dim, shards_of in shards:
        steps = jnp.exp(jax.random.uniform(jax.random.fold_in(own, dim), (shards_of,), jnp.float32, low / len(shards), largest / len(shards)))
        factor_of = factor_of * jnp.repeat(steps, extent[dim] // shards_of).reshape([-1 if axis == dim else 1 for axis in range(len(extent))])
    return factor_of


def normal_values(own_key, extent, width, limit, cuts=(), kind=jnp.bfloat16):
    values = jax.random.normal(own_key, extent, jnp.float32) * width
    if len(cuts) > 0:
        values = shard_levels(own_key, extent, cuts, -0.22, 0.18) * values
    return jnp.clip(values, min=-limit, max=limit).astype(kind)


def setup_inputs(seed: int = 0) -> dict:
    arg_keys = jax.random.split(jax.random.key(seed), 12)
    hidden_rows = normal_values(arg_keys[0], (SPAN, REQUESTS, D), 1.0, 6.0, ((0, 8), (1, 16)))
    norm_gain = jnp.clip(1.0 + 0.18 * jax.random.normal(arg_keys[1], (D,), jnp.float32), 0.1, 1.9)
    w_query = normal_values(arg_keys[2], (D, HEADS * HD), D ** -0.5, 0.0625, ((1, 8),))
    w_key = normal_values(arg_keys[3], (D, KVH * HD), D ** -0.5, 0.0625, ((1, 8),))
    w_value = normal_values(arg_keys[4], (D, KVH * HD), D ** -0.5, 0.0625, ((1, 8),))
    w_out = normal_values(arg_keys[5], (HEADS * HD, D), (HEADS * HD // 256) ** -0.5, 1.5, ((0, 8),))
    cache_keys = normal_values(arg_keys[6], (REQUESTS, PREFIX, KVH * HD), 1.0, 6.0, ((0, 16), (2, 8)))
    cache_values = normal_values(arg_keys[7], (REQUESTS, PREFIX, KVH * HD), 1.0, 6.0, ((0, 16), (2, 8)))
    slot_of_request = draw_slot_of_request(jax.random.fold_in(arg_keys[11], 71), 0)
    span_length = draw_span_length(jax.random.fold_in(arg_keys[11], 71), 0)
    prefix_length = draw_prefix_length(jax.random.fold_in(arg_keys[11], 71), 0)
    return dict(hidden_rows=hidden_rows, norm_gain=norm_gain, w_query=w_query, w_key=w_key, w_value=w_value, w_out=w_out, cache_keys=cache_keys, cache_values=cache_values, slot_of_request=slot_of_request, span_length=span_length, prefix_length=prefix_length)


rope_base = 500000.0
norm_eps = 1e-05
masked = -1e+30

def rotate(values, position):
    head_width = values.shape[-1]
    half_width = head_width // 2
    frequency = rope_base ** (-(jnp.arange(half_width, dtype=jnp.float32) * 2.0 / head_width))
    angles = position[..., None, None] * frequency
    cosine = jnp.cos(angles)
    sine_part = jnp.sin(angles)
    front_half = values[..., :half_width]
    back_half = values[..., half_width:]
    return jnp.concatenate([front_half * cosine - back_half * sine_part, back_half * cosine + front_half * sine_part], axis=-1)

def attend_one(inputs, cache_keys, cache_values):
    one_query, keys_new, values_new, slot_index, prefix_now, length_now = inputs
    span_rows = one_query.shape[0]
    groups = HEADS // KVH
    score_scale = HD ** (-0.5)
    keys_old = lax.dynamic_index_in_dim(cache_keys, slot_index.astype(jnp.int32), 0, keepdims=False)
    values_old = lax.dynamic_index_in_dim(cache_values, slot_index.astype(jnp.int32), 0, keepdims=False)
    grouped = one_query.reshape(span_rows, KVH, groups, HD).astype(jnp.float32)
    old_keys = keys_old.reshape(PREFIX, KVH, HD).astype(jnp.float32)
    old_values = values_old.reshape(PREFIX, KVH, HD).astype(jnp.float32)
    score_old = jnp.einsum('cgmd,pgd->gmcp', grouped, old_keys) * score_scale
    score_new = jnp.einsum('cgmd,jgd->gmcj', grouped, keys_new.astype(jnp.float32)) * score_scale
    keep_old = jnp.arange(PREFIX, dtype=jnp.int32) < prefix_now
    row_index = jnp.arange(span_rows, dtype=jnp.int32)
    keep_new = (row_index[None, :] < length_now) & (row_index[None, :] <= row_index[:, None])
    score_old = jnp.where(keep_old, score_old, masked)
    score_new = jnp.where(keep_new, score_new, masked)
    exp_old = jnp.exp(score_old)
    exp_new = jnp.exp(score_new)
    denominator = lax.optimization_barrier(jnp.sum(exp_old, axis=-1, keepdims=True)) + lax.optimization_barrier(jnp.sum(exp_new, axis=-1, keepdims=True))
    weight_old = (exp_old / denominator).astype(jnp.bfloat16).astype(jnp.float32)
    weight_new = (exp_new / denominator).astype(jnp.bfloat16).astype(jnp.float32)
    mixed = jnp.einsum('gmcp,pgd->cgmd', weight_old, old_values)
    mixed = mixed + jnp.einsum('gmcj,jgd->cgmd', weight_new, values_new.astype(jnp.float32))
    return mixed.astype(jnp.bfloat16).reshape(span_rows, HEADS * HD)

def reference(hidden_rows, norm_gain, w_query, w_key, w_value, w_out, cache_keys, cache_values, slot_of_request, span_length, prefix_length):
    floats = hidden_rows.astype(jnp.float32)
    normed = (floats * lax.rsqrt(lax.optimization_barrier(jnp.mean(floats * floats, axis=-1, keepdims=True)) + norm_eps) * norm_gain).astype(jnp.bfloat16)
    flat_rows = normed.reshape(SPAN * REQUESTS, D)
    positions = (prefix_length[None, :] + jnp.arange(SPAN, dtype=jnp.int32)[:, None]).astype(jnp.float32)
    queries = jnp.dot(flat_rows, w_query, preferred_element_type=jnp.float32).reshape(SPAN, REQUESTS, HEADS, HD)
    queries = rotate(queries, positions).astype(jnp.bfloat16)
    keys_new = jnp.dot(flat_rows, w_key, preferred_element_type=jnp.float32).reshape(SPAN, REQUESTS, KVH, HD)
    keys_new = rotate(keys_new, positions).astype(jnp.bfloat16)
    values_new = jnp.dot(flat_rows, w_value, preferred_element_type=jnp.float32).astype(jnp.bfloat16).reshape(SPAN, REQUESTS, KVH, HD)
    inputs = (jnp.transpose(queries, (1, 0, 2, 3)), jnp.transpose(keys_new, (1, 0, 2, 3)), jnp.transpose(values_new, (1, 0, 2, 3)), slot_of_request, prefix_length, span_length)
    heads_out = lax.map(lambda one_input: attend_one(one_input, cache_keys, cache_values), inputs)
    heads_out = jnp.transpose(heads_out, (1, 0, 2)).reshape(SPAN * REQUESTS, HEADS * HD)
    result = jnp.dot(heads_out, w_out, preferred_element_type=jnp.float32)
    return result.astype(jnp.bfloat16).reshape(SPAN, REQUESTS, D)
```

```python
import functools

import jax
import jax.numpy as jnp
from jax import lax
from jax.experimental import pallas as pl
from jax.experimental.pallas import tpu as pltpu
from jax.sharding import PartitionSpec as P

HD = 128
rope_base = 500000.0
norm_eps = 1e-05
masked = -1e30
log2e = 1.4426950408889634
MESH = pl.DeviceIdType.MESH


def peers():
    n = lax.axis_size("tensor")
    t = lax.axis_index("tensor")
    core = lax.rem(t, 2)
    return t, core, lax.rem(t + 2, n), lax.rem(t + n - 2, n), t + 1 - 2 * core


def greet(devices):
    barrier = pltpu.get_barrier_semaphore()
    for device in devices:
        pl.semaphore_signal(barrier, inc=1, device_id={"tensor": device}, device_id_type=MESH)
    pl.semaphore_wait(barrier, len(devices))


def remote(source, target, send_sem, recv_sem, device):
    return pltpu.make_async_remote_copy(
        src_ref=source,
        dst_ref=target,
        send_sem=send_sem,
        recv_sem=recv_sem,
        device_id={"tensor": device},
        device_id_type=MESH,
    )


TO_RIGHT, TO_LEFT, TO_SIB, ON_RIGHT, ON_LEFT, SIB_LEFT, SIB_RIGHT, SIB_FAR0, SIB_FAR1 = range(9)


def gather_project_kernel(
    chunks, x_ref, wq_ref, wk_ref, wv_ref, cos_ref, sin_ref, out_ref,
    rows, weights, total, w_sem, x_sem, send_sem, recv_sem,
):
    t, core, right, left, sib = peers()
    n = lax.axis_size("tensor")
    block = x_ref.shape[1]
    width = rows.shape[-1]
    q_width, kv_width = wq_ref.shape[1], wk_ref.shape[1]
    far = lax.rem(t + n // 2, n)

    def at(device):
        return pl.ds(pl.multiple_of(device * block, block), block)

    def piece(k, device):
        return rows.at[k, :, at(device), :]

    def half(k, which, device):
        return rows.at[k, which, at(device), :]

    def message(kind, k, view, device):
        return remote(view, view, send_sem.at[kind, k], recv_sem.at[kind, k], device)

    x_copies = [
        pltpu.make_async_copy(
            x_ref.at[:, :, pl.ds(k * width, width)], piece(k, t), x_sem.at[k]
        )
        for k in range(chunks)
    ]
    for copy in x_copies:
        copy.start()
    w_copies = []
    for index, (ref, start, size) in enumerate(
        ((wq_ref, 0, q_width), (wk_ref, q_width, kv_width), (wv_ref, q_width + kv_width, kv_width))
    ):
        copy = pltpu.make_async_copy(ref, weights.at[:, pl.ds(start, size)], w_sem.at[index])
        w_copies.append(copy)
    greet((right, left, sib))
    for k in range(chunks):
        x_copies[k].wait()
        message(TO_RIGHT, k, piece(k, t), right).start()
        message(TO_LEFT, k, piece(k, t), left).start()
        message(TO_SIB, k, piece(k, t), sib).start()
    for copy in w_copies:
        copy.start()
    total[...] = jnp.zeros_like(total)

    def onward(k, carry):
        message(TO_RIGHT, k, piece(k, left), right).wait_recv()
        message(ON_RIGHT, k, half(k, 0, left), right).start()
        message(SIB_LEFT, k, piece(k, left), sib).start()
        message(TO_LEFT, k, piece(k, right), left).wait_recv()
        message(ON_LEFT, k, half(k, 1, right), left).start()
        message(SIB_RIGHT, k, piece(k, right), sib).start()
        return carry

    lax.fori_loop(0, chunks, onward, 0)
    for copy in w_copies:
        copy.wait()
    sib_left, sib_right, sib_far = (
        left + 1 - 2 * core, right + 1 - 2 * core, far + 1 - 2 * core
    )

    def multiply(k, carry):
        @pl.when(k < chunks)
        def _():
            message(ON_RIGHT, k, half(k, 0, far), right).wait_recv()
            message(SIB_FAR0, k, half(k, 0, far), sib).start()
            message(ON_LEFT, k, half(k, 1, far), left).wait_recv()
            message(SIB_FAR1, k, half(k, 1, far), sib).start()

        @pl.when(k > 0)
        def _():
            j = k - 1
            message(TO_SIB, j, piece(j, sib), sib).wait_recv()
            message(SIB_LEFT, j, piece(j, sib_left), sib).wait_recv()
            message(SIB_RIGHT, j, piece(j, sib_right), sib).wait_recv()
            message(SIB_FAR0, j, half(j, 0, sib_far), sib).wait_recv()
            message(SIB_FAR1, j, half(j, 1, sib_far), sib).wait_recv()
            depth = pl.ds(pl.multiple_of(j * width, width), width)
            for r in range(rows.shape[1]):
                total[r] += jnp.dot(
                    rows[j, r], weights[depth, :], preferred_element_type=jnp.float32
                )

        return carry

    lax.fori_loop(0, chunks + 1, multiply, 0)
    half_head = HD // 2
    for r in range(rows.shape[1]):
        cosine, sine = cos_ref[r], sin_ref[r]
        for h in range((q_width + kv_width) // HD):
            columns = pl.ds(h * HD, HD)
            value = total[r, :, columns]
            value = value * cosine + pltpu.roll(value, half_head, axis=1) * sine
            if h < q_width // HD:
                value = value * (HD ** (-0.5) * log2e)
            out_ref[r, :, columns] = value.astype(out_ref.dtype)
        columns = pl.ds(q_width + kv_width, kv_width)
        out_ref[r, :, columns] = total[r, :, columns].astype(out_ref.dtype)

    def drain(k, carry):
        for kind in range(3):
            message(kind, k, piece(k, t), (right, left, sib)[kind]).wait_send()
        message(ON_RIGHT, k, half(k, 0, left), right).wait_send()
        message(ON_LEFT, k, half(k, 1, right), left).wait_send()
        message(SIB_LEFT, k, piece(k, left), sib).wait_send()
        message(SIB_RIGHT, k, piece(k, right), sib).wait_send()
        message(SIB_FAR0, k, half(k, 0, far), sib).wait_send()
        message(SIB_FAR1, k, half(k, 1, far), sib).wait_send()
        return carry

    lax.fori_loop(0, chunks, drain, 0)


def gather_project(x, wq, wk, wv, cosine, sine, chunks=8):
    requests, block, depth = x.shape
    n = lax.axis_size("tensor")
    width = wq.shape[1] + wk.shape[1] + wv.shape[1]
    any_space = pl.BlockSpec(memory_space=pl.ANY)
    vmem = pl.BlockSpec(memory_space=pltpu.VMEM)
    return pl.pallas_call(
        functools.partial(gather_project_kernel, chunks),
        out_shape=jax.ShapeDtypeStruct((requests, block * n, width), jnp.bfloat16),
        in_specs=[any_space] * 4 + [vmem] * 2,
        out_specs=vmem,
        scratch_shapes=[
            pltpu.VMEM((chunks, requests, block * n, depth // chunks), jnp.bfloat16),
            pltpu.VMEM((depth, width), jnp.bfloat16),
            pltpu.VMEM((requests, block * n, width), jnp.float32),
            pltpu.SemaphoreType.DMA((3,)),
            pltpu.SemaphoreType.DMA((chunks,)),
            pltpu.SemaphoreType.DMA((9, chunks)),
            pltpu.SemaphoreType.DMA((9, chunks)),
        ],
        compiler_params=pltpu.CompilerParams(
            collective_id=0, has_side_effects=True, vmem_limit_bytes=48 << 20
        ),
        name="gather_project",
    )(x, wq, wk, wv, cosine, sine)


def attend_kernel(order_ref, prefix_ref, span_ref, x_ref, k_ref, v_ref, out_ref):
    packet = pl.program_id(0)
    span_rows = x_ref.shape[1]
    prefix_rows = k_ref.shape[1]
    q_width = out_ref.shape[2]
    prefix, span = prefix_ref[packet], span_ref[packet]
    keys_new = x_ref[0, :, q_width : q_width + HD]
    values_new = x_ref[0, :, q_width + HD :]
    old_column = lax.broadcasted_iota(jnp.int32, (1, prefix_rows), 1)
    old_bias = jnp.where(old_column < prefix, 0.0, masked)
    row = lax.broadcasted_iota(jnp.int32, (span_rows, span_rows), 0)
    column = lax.broadcasted_iota(jnp.int32, (span_rows, span_rows), 1)
    new_bias = jnp.where((column <= row) & (column < span), 0.0, masked)
    contract = (((1,), (1,)), ((), ()))
    for h in range(q_width // HD):
        query = x_ref[0, :, h * HD : (h + 1) * HD]
        old = (
            lax.dot_general(query, k_ref[0], contract, preferred_element_type=jnp.float32)
            + old_bias
        )
        new = (
            lax.dot_general(query, keys_new, contract, preferred_element_type=jnp.float32)
            + new_bias
        )
        top = jnp.maximum(
            jnp.max(old, axis=1, keepdims=True), jnp.max(new, axis=1, keepdims=True)
        )
        old = jnp.exp2(old - top)
        new = jnp.exp2(new - top)
        weight_sum = jnp.sum(old, axis=1, keepdims=True) + jnp.sum(new, axis=1, keepdims=True)
        mixed = jnp.dot(old.astype(jnp.bfloat16), v_ref[0], preferred_element_type=jnp.float32)
        mixed += jnp.dot(
            new.astype(jnp.bfloat16), values_new, preferred_element_type=jnp.float32
        )
        out_ref[0, :, h * HD : (h + 1) * HD] = (mixed / weight_sum).astype(out_ref.dtype)


def attend(packets, cache_keys, cache_values, order, prefix, span, q_width):
    count, span_rows, width = packets.shape
    _, prefix_rows, kv_width = cache_keys.shape
    cache = pl.BlockSpec((1, prefix_rows, kv_width), lambda i, order, p, s: (order[i], 0, 0))
    return pl.pallas_call(
        attend_kernel,
        out_shape=jax.ShapeDtypeStruct((count, span_rows, q_width), jnp.bfloat16),
        grid_spec=pltpu.PrefetchScalarGridSpec(
            num_scalar_prefetch=3,
            grid=(count,),
            in_specs=[
                pl.BlockSpec((1, span_rows, width), lambda i, *_: (i, 0, 0)),
                cache,
                cache,
            ],
            out_specs=pl.BlockSpec((1, span_rows, q_width), lambda i, *_: (i, 0, 0)),
        ),
        compiler_params=pltpu.CompilerParams(vmem_limit_bytes=48 << 20),
        name="attend",
    )(order, prefix, span, packets, cache_keys, cache_values)


SWAP, FAR_RIGHT, FAR_LEFT, SUM_RIGHT, SUM_LEFT = range(5)


def project_reduce_kernel(
    chunks, heads_ref, w_ref, out_ref,
    weights, mine, swap_out, swap_in, far_out, far_in, sum_out, sum_in, w_sem, send_sem, recv_sem,
):
    t, core, right, left, sib = peers()
    requests, block, _ = out_ref.shape
    chips = lax.axis_size("tensor") // 2
    width = swap_out.shape[-1]
    z = t // 2
    z_right, z_left, z_far = right // 2, left // 2, lax.rem(z + chips // 2, chips)

    def message(kind, j, source, target, device):
        return remote(source, target, send_sem.at[kind, j], recv_sem.at[kind, j], device)

    def swap(j):
        return message(SWAP, j, swap_out.at[j], swap_in.at[j], sib)

    def far_right(j):
        return message(FAR_RIGHT, j, far_out.at[j, 0], far_in.at[j, 0], right)

    def far_left(j):
        return message(FAR_LEFT, j, far_out.at[j, 1], far_in.at[j, 1], left)

    def sum_right(j):
        return message(SUM_RIGHT, j, sum_out.at[j, 0], sum_in.at[j, 0], right)

    def sum_left(j):
        return message(SUM_LEFT, j, sum_out.at[j, 1], sum_in.at[j, 1], left)

    w_copies = [
        pltpu.make_async_copy(
            w_ref.at[:, pl.ds(j * width, width)], weights.at[j], w_sem.at[j]
        )
        for j in range(chunks)
    ]
    for copy in w_copies:
        copy.start()
    greet((right, left, sib))

    def columns(j):
        return pl.ds(pl.multiple_of(j * width, width), width)

    def step(j, carry):
        @pl.when(j < chunks)
        def _():
            pltpu.make_async_copy(w_ref.at[:, columns(j)], weights.at[j], w_sem.at[j]).wait()
            for r in range(requests):
                part = jnp.dot(
                    heads_ref[r], weights[j], preferred_element_type=jnp.float32
                ).reshape(chips, 2, block, width)
                keep = jnp.where(core == 0, part[:, 0], part[:, 1])
                give = jnp.where(core == 0, part[:, 1], part[:, 0])
                mine[j, r] = keep
                swap_out[j, r] = give.astype(jnp.bfloat16)
            swap(j).start()

        @pl.when((j > 0) & (j <= chunks))
        def _():
            i = j - 1
            swap(i).wait_recv()
            for r in range(requests):
                mine[i, r] = mine[i, r] + swap_in[i, r].astype(jnp.float32)
            far_out[i, 0] = mine[i, 0, z_far].astype(jnp.bfloat16)
            far_out[i, 1] = mine[i, 1, z_far].astype(jnp.bfloat16)
            far_right(i).start()
            far_left(i).start()

        @pl.when(j > 1)
        def _():
            i = j - 2
            sum_out[i, 0, 1] = mine[i, 1, z_right].astype(jnp.bfloat16)
            sum_out[i, 1, 0] = mine[i, 0, z_left].astype(jnp.bfloat16)
            far_right(i).wait_recv()
            sum_out[i, 0, 0] = (
                mine[i, 0, z_right] + far_in[i, 0].astype(jnp.float32)
            ).astype(jnp.bfloat16)
            sum_right(i).start()
            far_left(i).wait_recv()
            sum_out[i, 1, 1] = (
                mine[i, 1, z_left] + far_in[i, 1].astype(jnp.float32)
            ).astype(jnp.bfloat16)
            sum_left(i).start()

        return carry

    lax.fori_loop(0, chunks + 2, step, 0)

    def finish(j, carry):
        sum_right(j).wait_recv()
        sum_left(j).wait_recv()
        for r in range(requests):
            out_ref[r, :, columns(j)] = (
                mine[j, r, z]
                + sum_in[j, 0, r].astype(jnp.float32)
                + sum_in[j, 1, r].astype(jnp.float32)
            ).astype(jnp.bfloat16)
        return carry

    lax.fori_loop(0, chunks, finish, 0)

    def drain(j, carry):
        swap(j).wait_send()
        far_right(j).wait_send()
        far_left(j).wait_send()
        sum_right(j).wait_send()
        sum_left(j).wait_send()
        return carry

    lax.fori_loop(0, chunks, drain, 0)


def project_reduce(heads, w_out, chunks=8):
    requests, span_rows, depth = heads.shape
    n = lax.axis_size("tensor")
    block = span_rows // n
    features = w_out.shape[1]
    width = features // chunks
    bf16, f32 = jnp.bfloat16, jnp.float32
    return pl.pallas_call(
        functools.partial(project_reduce_kernel, chunks),
        out_shape=jax.ShapeDtypeStruct((requests, block, features), bf16),
        in_specs=[pl.BlockSpec(memory_space=pltpu.VMEM), pl.BlockSpec(memory_space=pl.ANY)],
        out_specs=pl.BlockSpec(memory_space=pltpu.VMEM),
        scratch_shapes=[
            pltpu.VMEM((chunks, depth, width), bf16),
            pltpu.VMEM((chunks, requests, n // 2, block, width), f32),
            pltpu.VMEM((chunks, requests, n // 2, block, width), bf16),
            pltpu.VMEM((chunks, requests, n // 2, block, width), bf16),
            pltpu.VMEM((chunks, 2, block, width), bf16),
            pltpu.VMEM((chunks, 2, block, width), bf16),
            pltpu.VMEM((chunks, 2, requests, block, width), bf16),
            pltpu.VMEM((chunks, 2, requests, block, width), bf16),
            pltpu.SemaphoreType.DMA((chunks,)),
            pltpu.SemaphoreType.DMA((5, chunks)),
            pltpu.SemaphoreType.DMA((5, chunks)),
        ],
        compiler_params=pltpu.CompilerParams(
            collective_id=1, has_side_effects=True, vmem_limit_bytes=52 << 20
        ),
        name="project_reduce",
    )(heads, w_out)


def exchange(first, second, mask):
    size = lax.axis_size("dp")

    def swap(value, other):
        if other == 0:
            return value
        return lax.ppermute(value, "dp", [(i, i ^ other) for i in range(size)])

    def branch(other):
        return lambda a, b: (swap(a, 1), swap(b, other))

    return lax.switch(mask, [branch(other) for other in range(size)], first, second)


def local(
    hidden_rows, norm_gain, w_query, w_key, w_value, w_out, cache_keys, cache_values,
    slot_of_request, span_length, prefix_length,
):
    per_device = hidden_rows.shape[1]
    q_width = w_query.shape[1]
    data_index = lax.axis_index("dp")
    tensor_size = lax.axis_size("tensor")
    mine = lax.dynamic_slice_in_dim(slot_of_request, data_index * per_device, per_device)
    masks = jnp.bitwise_xor(mine // per_device, data_index)
    near = jnp.where(masks[0] == 1, 0, 1)
    mask = jnp.where(masks[0] == 1, masks[1], masks[0])

    floats = hidden_rows.astype(jnp.float32)
    normed = (
        floats * lax.rsqrt(jnp.mean(floats * floats, axis=-1, keepdims=True) + norm_eps) * norm_gain
    ).astype(jnp.bfloat16)
    normed = jnp.transpose(normed, (1, 0, 2))

    span_rows = hidden_rows.shape[0] * tensor_size
    prefix_here = lax.dynamic_slice_in_dim(prefix_length, data_index * per_device, per_device)
    frequency = rope_base ** (-(jnp.arange(HD // 2, dtype=jnp.float32) * 2.0 / HD))
    positions = (prefix_here[:, None] + jnp.arange(span_rows, dtype=jnp.int32)[None, :]).astype(
        jnp.float32
    )
    angles = positions[:, :, None] * frequency
    cosine, sine = jnp.cos(angles), jnp.sin(angles)
    cosine = jnp.concatenate([cosine, cosine], axis=-1)
    sine = jnp.concatenate([-sine, sine], axis=-1)
    packed = gather_project(normed, w_query, w_key, w_value, cosine, sine)

    flip = near == 1
    near_packet = jnp.where(flip, packed[1], packed[0])
    other_packet = jnp.where(flip, packed[0], packed[1])
    near_in, other_in = exchange(near_packet, other_packet, mask)

    slots = data_index * per_device + jnp.arange(per_device, dtype=jnp.int32)
    match = slot_of_request[None, :] == slots[:, None]
    request_of = jnp.sum(
        jnp.where(match, jnp.arange(slot_of_request.shape[0], dtype=jnp.int32)[None, :], 0), axis=1
    )
    slot_prefix = jnp.sum(jnp.where(match, prefix_length[None, :], 0), axis=1)
    slot_span = jnp.sum(jnp.where(match, span_length[None, :], 0), axis=1)
    from_near = jnp.bitwise_xor(request_of // per_device, data_index) == 1
    near_slot = jnp.where(from_near[0], 0, 1).astype(jnp.int32)
    order = jnp.stack([near_slot, 1 - near_slot])
    swapped = near_slot == 1
    prefix = jnp.where(swapped, slot_prefix[::-1], slot_prefix)
    span = jnp.where(swapped, slot_span[::-1], slot_span)
    mixed = attend(
        jnp.stack([near_in, other_in]), cache_keys, cache_values, order, prefix, span, q_width
    )
    near_back, other_back = exchange(mixed[0], mixed[1], mask)
    heads = jnp.stack(
        [jnp.where(flip, other_back, near_back), jnp.where(flip, near_back, other_back)]
    )
    result = project_reduce(heads, w_out)
    return jnp.transpose(result, (1, 0, 2))


def solution(mesh):
    placed = (
        P("tensor", "dp", None),
        P(),
        P(None, "tensor"),
        P(None, "tensor"),
        P(None, "tensor"),
        P("tensor", None),
        P("dp", None, "tensor"),
        P("dp", None, "tensor"),
        P(),
        P(),
        P(),
    )
    return jax.shard_map(
        local, mesh=mesh, in_specs=placed, out_specs=P("tensor", "dp", None), check_vma=False
    )
```

```python
import functools

import jax
import jax.numpy as jnp
from jax import lax
from jax.experimental import pallas as pl
from jax.experimental.pallas import tpu as pltpu
from jax.sharding import PartitionSpec as P

HD = 128
rope_base = 500000.0
norm_eps = 1e-05
masked = -1e30
log2e = 1.4426950408889634
VMEM_LIMIT = 62 << 20
MESH = pl.DeviceIdType.MESH


def peers():
    n = lax.axis_size("tensor")
    t = lax.axis_index("tensor")
    core = lax.rem(t, 2)
    return t, core, lax.rem(t + 2, n), lax.rem(t + n - 2, n), t + 1 - 2 * core


def greet(devices):
    barrier = pltpu.get_barrier_semaphore()
    for device in devices:
        pl.semaphore_signal(barrier, inc=1, device_id=device, device_id_type=MESH)
    pl.semaphore_wait(barrier, len(devices))


def remote(source, target, sems, index, device):
    return pltpu.make_async_remote_copy(
        src_ref=source,
        dst_ref=target,
        send_sem=sems.at[(0, *index)],
        recv_sem=sems.at[(1, *index)],
        device_id=device,
        device_id_type=MESH,
    )


TO_RIGHT, TO_LEFT, TO_SIB, ONWARD, SIB_LEFT, SIB_RIGHT, SIB_FAR = range(7)
SWAP, FAR, SUM_RIGHT, SUM_LEFT = range(4)
NEIGHBOURS, FAR_BLOCK, PRODUCT = 2, 4, 5
CHIP_SUM, PASS_ON, RESULT = 1, 3, 5


def layer_kernel(
    plan, flags_ref, lengths_ref, x_ref, cos_ref, sin_ref, wq_ref, wk_ref, wv_ref, wo_ref,
    ck_ref, cv_ref, out_ref,
    rows, hop, weights, weights_out, cache_k, cache_v, total, packed, heads, back, home,
    mine, swap_out, swap_in, far_out, far_in, sum_out, sum_in,
    local_sem, near_sem, hop_sem, gather_sem, near_back_sem, back_sem, reduce_sem,
):
    chunks, stages, q_heads = plan
    t, core, right, left, sib = peers()
    n = lax.axis_size("tensor")
    chips = n // 2
    far = lax.rem(t + chips, n)
    z = t // 2
    z_right, z_left, z_far = right // 2, left // 2, far // 2
    d = lax.axis_index("dp")
    block = x_ref.shape[1]
    span_rows = block * n
    width = rows.shape[-1]
    q_width, kv_width = wq_ref.shape[1], wk_ref.shape[1]
    bf16, f32 = jnp.bfloat16, jnp.float32
    total_chunks = 2 * chunks

    def flipped(bit):
        size = 1 << bit
        return {"dp": d + size - 2 * size * lax.rem(d // size, 2)}

    def across(device):
        return {"tensor": device}

    def stage_device(s):
        return flipped(stages - 1 - s)

    def at(device):
        return pl.ds(pl.multiple_of(device * block, block), block)

    def columns(k):
        return pl.ds(pl.multiple_of(k * width, width), width)

    def head_columns(h):
        return pl.ds(pl.multiple_of(h * HD, HD), HD)

    def near(k):
        return remote(
            x_ref.at[0, :, columns(k)], rows.at[0, k, at(t), :], near_sem, (k,), flipped(0)
        )

    def hop_source(s, k):
        return x_ref.at[1, :, columns(k)] if s == 0 else hop.at[s - 1, k]

    def hops(s, k):
        return remote(hop_source(s, k), hop.at[s, k], hop_sem, (s, k), stage_device(s))

    def gather(kind, q, owner, device):
        view = rows.at[q // chunks, lax.rem(q, chunks), at(owner), :]
        return remote(view, view, gather_sem, (kind, q), across(device))

    def onward(q):
        odd = lax.rem(q, 2)
        return gather(
            ONWARD, q, left * (1 - odd) + right * odd, right * (1 - odd) + left * odd
        )

    def near_back(h):
        return remote(
            heads.at[0, :, head_columns(h)], home.at[0, :, head_columns(h)],
            near_back_sem, (h,), flipped(0),
        )

    def back_source(s, h):
        return heads.at[1, :, head_columns(h)] if s == 0 else back.at[s - 1, h]

    def backs(s, h):
        return remote(back_source(s, h), back.at[s, h], back_sem, (s, h), stage_device(s))

    def swap(r):
        return remote(swap_out.at[r], swap_in.at[r], reduce_sem, (SWAP, r), across(sib))

    def far_sum(r):
        odd = lax.rem(r, 2)
        return remote(
            far_out.at[r], far_in.at[r], reduce_sem, (FAR, r),
            across(right * (1 - odd) + left * odd),
        )

    def sum_right(r):
        return remote(
            sum_out.at[r, 0], sum_in.at[r, 0], reduce_sem, (SUM_RIGHT, r), across(right)
        )

    def sum_left(r):
        return remote(
            sum_out.at[r, 1], sum_in.at[r, 1], reduce_sem, (SUM_LEFT, r), across(left)
        )

    def weight_copy(index):
        ref = (wq_ref, wk_ref, wv_ref)[index]
        start = (0, q_width, q_width + kv_width)[index]
        return pltpu.make_async_copy(
            ref, weights.at[:, pl.ds(start, ref.shape[1])], local_sem.at[index]
        )

    def out_copy(j):
        return pltpu.make_async_copy(
            wo_ref.at[:, columns(j)], weights_out.at[j], local_sem.at[5 + j]
        )

    cache_copies = (
        pltpu.make_async_copy(ck_ref, cache_k, local_sem.at[3]),
        pltpu.make_async_copy(cv_ref, cache_v, local_sem.at[4]),
    )

    greet([across(right), across(left), across(sib)] + [flipped(b) for b in range(stages)])
    for k in range(chunks):
        near(k).start()
    for k in range(chunks):
        hops(0, k).start()
    for index in range(3):
        weight_copy(index).start()
    for copy in cache_copies:
        copy.start()
    for j in range(chunks):
        out_copy(j).start()
    total[...] = jnp.zeros_like(total)

    def mix(flag, taken, kept):
        return (taken.astype(f32) * flag + kept.astype(f32) * (1.0 - flag)).astype(bf16)

    sib_of = 1 - 2 * core
    attend_near = chunks + PRODUCT
    attend_other = total_chunks + PRODUCT
    reduce_near = attend_near + q_heads + 1
    reduce_other = max(attend_other + q_heads + stages, reduce_near + chunks)
    last = reduce_other + chunks + RESULT
    contract = (((1,), (1,)), ((), ()))

    def within(value, low, high):
        return (value >= low) & (value < high)

    def reduce_index(tick):
        first = tick - reduce_near
        second = tick - reduce_other
        on_first, on_second = within(first, 0, chunks), within(second, 0, chunks)
        late = lax.select(second >= 0, 1, 0)
        return first * (1 - late) + (second + chunks) * late, on_first | on_second

    def tick_body(tick, carry):
        @pl.when(tick < chunks)
        def _():
            near(tick).wait_recv()

        @pl.when(tick < total_chunks)
        def _():
            gather(TO_RIGHT, tick, t, right).start()
            gather(TO_LEFT, tick, t, left).start()
            gather(TO_SIB, tick, t, sib).start()

        @pl.when(within(tick - NEIGHBOURS, 0, total_chunks))
        def _():
            q = tick - NEIGHBOURS
            gather(TO_RIGHT, q, left, right).wait_recv()
            gather(TO_LEFT, q, right, left).wait_recv()
            onward(q).start()
            gather(SIB_LEFT, q, left, sib).start()
            gather(SIB_RIGHT, q, right, sib).start()

        @pl.when(within(tick - FAR_BLOCK, 0, total_chunks))
        def _():
            q = tick - FAR_BLOCK
            onward(q).wait_recv()
            gather(SIB_FAR, q, far, sib).start()

        for s in range(stages):
            k = tick - (chunks - 2 * stages + 2 * s)

            @pl.when(within(k, 0, chunks))
            def _(s=s, k=k):
                hops(s, k).wait_recv()
                flag = flags_ref[s]
                value = mix(flag, hop[s, k], hop_source(s, k)[...])
                if s < stages - 1:
                    hop[s, k] = value
                    hops(s + 1, k).start()
                else:
                    rows[1, k, at(t), :] = value

        @pl.when(tick == PRODUCT - 1)
        def _():
            for copy in cache_copies:
                copy.wait()
            flag = flags_ref[stages]
            for cache in (cache_k, cache_v):
                first, second = cache[0], cache[1]
                cache[0] = mix(flag, second, first)
                cache[1] = mix(flag, first, second)
            for index in range(3):
                weight_copy(index).wait()

        r, on = reduce_index(tick - PASS_ON)

        @pl.when(on)
        def _():
            odd = lax.rem(r, 2).astype(f32)
            far_sum(r).wait_recv()
            passed = far_in[r].astype(f32)
            sum_out[r, 0] = (mine[r, z_right].astype(f32) + passed * (1.0 - odd)).astype(bf16)
            sum_out[r, 1] = (mine[r, z_left].astype(f32) + passed * odd).astype(bf16)
            sum_right(r).start()
            sum_left(r).start()

        r, on = reduce_index(tick - CHIP_SUM)

        @pl.when(on)
        def _():
            swap(r).wait_recv()
            value = mine[r].astype(f32) + swap_in[r].astype(f32)
            mine[r] = value.astype(bf16)
            far_out[r] = mine[r, z_far]
            far_sum(r).start()

        r, on = reduce_index(tick)

        @pl.when(on)
        def _():
            p, j = r // chunks, lax.rem(r, chunks)

            @pl.when(r == 0)
            def _():
                for h in range(q_heads):
                    near_back(h).wait_recv()

            @pl.when(r < chunks)
            def _():
                out_copy(j).wait()

            part = jnp.dot(home[p], weights_out[j], preferred_element_type=f32)
            part = part.reshape(chips, 2, block, width)
            mine[r] = jnp.where(core == 0, part[:, 0], part[:, 1]).astype(bf16)
            swap_out[r] = jnp.where(core == 0, part[:, 1], part[:, 0]).astype(bf16)
            swap(r).start()

        @pl.when(within(tick - PRODUCT, 0, total_chunks))
        def _():
            q = tick - PRODUCT
            p, k = q // chunks, lax.rem(q, chunks)
            gather(TO_SIB, q, sib, sib).wait_recv()
            gather(SIB_LEFT, q, left + sib_of, sib).wait_recv()
            gather(SIB_RIGHT, q, right + sib_of, sib).wait_recv()
            gather(SIB_FAR, q, far + sib_of, sib).wait_recv()
            total[...] += jnp.dot(rows[p, k], weights[columns(k), :], preferred_element_type=f32)

            @pl.when(k == chunks - 1)
            def _():
                cosine, sine = cos_ref[p], sin_ref[p]
                for h in range((q_width + kv_width) // HD):
                    place = pl.ds(h * HD, HD)
                    value = total[:, place]
                    value = value * cosine + pltpu.roll(value, HD // 2, axis=1) * sine
                    if h < q_heads:
                        value = value * (HD ** (-0.5) * log2e)
                    packed[p, :, place] = value.astype(bf16)
                place = pl.ds(q_width + kv_width, kv_width)
                packed[p, :, place] = total[:, place].astype(bf16)
                total[...] = jnp.zeros_like(total)

        @pl.when(
            within(tick - attend_near, 0, q_heads) | within(tick - attend_other, 0, q_heads)
        )
        def _():
            late = lax.select(tick >= attend_other, 1, 0)
            p = late
            h = tick - attend_near * (1 - late) - attend_other * late
            prefix, span = lengths_ref[p], lengths_ref[2 + p]
            prefix_rows = cache_k.shape[1]
            keys_new = packed[p, :, pl.ds(q_width, kv_width)]
            values_new = packed[p, :, pl.ds(q_width + kv_width, kv_width)]
            old_column = lax.broadcasted_iota(jnp.int32, (1, prefix_rows), 1)
            old_bias = jnp.where(old_column < prefix, 0.0, masked)
            row = lax.broadcasted_iota(jnp.int32, (span_rows, span_rows), 0)
            column = lax.broadcasted_iota(jnp.int32, (span_rows, span_rows), 1)
            new_bias = jnp.where((column <= row) & (column < span), 0.0, masked)
            query = packed[p, :, head_columns(h)]
            old = lax.dot_general(query, cache_k[p], contract, preferred_element_type=f32)
            old = old + old_bias
            new = lax.dot_general(query, keys_new, contract, preferred_element_type=f32)
            new = new + new_bias
            top = jnp.maximum(
                jnp.max(old, axis=1, keepdims=True), jnp.max(new, axis=1, keepdims=True)
            )
            old = jnp.exp2(old - top)
            new = jnp.exp2(new - top)
            weight_sum = jnp.sum(old, axis=1, keepdims=True) + jnp.sum(
                new, axis=1, keepdims=True
            )
            mixed = jnp.dot(old.astype(bf16), cache_v[p], preferred_element_type=f32)
            mixed += jnp.dot(new.astype(bf16), values_new, preferred_element_type=f32)
            heads[p, :, head_columns(h)] = (mixed / weight_sum).astype(bf16)

            @pl.when(p == 0)
            def _():
                near_back(h).start()

            @pl.when(p == 1)
            def _():
                backs(0, h).start()

        for s in range(stages):
            h = tick - (attend_other + 1 + s)

            @pl.when(within(h, 0, q_heads))
            def _(s=s, h=h):
                backs(s, h).wait_recv()
                value = mix(flags_ref[s], back[s, h], back_source(s, h)[...])
                if s < stages - 1:
                    back[s, h] = value
                    backs(s + 1, h).start()
                else:
                    home[1, :, head_columns(h)] = value

        r, on = reduce_index(tick - RESULT)

        @pl.when(on)
        def _():
            p, j = r // chunks, lax.rem(r, chunks)
            sum_right(r).wait_recv()
            sum_left(r).wait_recv()
            out_ref[p, :, columns(j)] = (
                mine[r, z].astype(f32) + sum_in[r, 0].astype(f32) + sum_in[r, 1].astype(f32)
            ).astype(bf16)

        return carry

    lax.fori_loop(0, last, tick_body, 0)

    def drain_rows(k, carry):
        near(k).wait_send()
        for s in range(stages):
            hops(s, k).wait_send()
        return carry

    def drain_blocks(q, carry):
        gather(TO_RIGHT, q, t, right).wait_send()
        gather(TO_LEFT, q, t, left).wait_send()
        gather(TO_SIB, q, t, sib).wait_send()
        onward(q).wait_send()
        gather(SIB_LEFT, q, left, sib).wait_send()
        gather(SIB_RIGHT, q, right, sib).wait_send()
        gather(SIB_FAR, q, far, sib).wait_send()
        swap(q).wait_send()
        far_sum(q).wait_send()
        sum_right(q).wait_send()
        sum_left(q).wait_send()
        return carry

    def drain_heads(h, carry):
        near_back(h).wait_send()
        for s in range(stages):
            backs(s, h).wait_send()
        return carry

    lax.fori_loop(0, chunks, drain_rows, 0)
    lax.fori_loop(0, total_chunks, drain_blocks, 0)
    lax.fori_loop(0, q_heads, drain_heads, 0)


def layer(flags, lengths, x, cosine, sine, wq, wk, wv, wo, cache_keys, cache_values, chunks=8):
    packets, block, depth = x.shape
    n, dp = lax.axis_size("tensor"), lax.axis_size("dp")
    stages = dp.bit_length() - 1
    q_width, kv_width = wq.shape[1], wk.shape[1]
    all_width = q_width + 2 * kv_width
    q_heads = q_width // HD
    rows, width = block * n, depth // chunks
    bf16, f32 = jnp.bfloat16, jnp.float32
    any_space = pl.BlockSpec(memory_space=pl.ANY)
    smem = pl.BlockSpec(memory_space=pltpu.SMEM)
    vmem = pl.BlockSpec(memory_space=pltpu.VMEM)
    steps = packets * chunks
    dma = pltpu.SemaphoreType.DMA
    return pl.pallas_call(
        functools.partial(layer_kernel, (chunks, stages, q_heads)),
        out_shape=jax.ShapeDtypeStruct((packets, block, depth), bf16),
        in_specs=[smem] * 2 + [vmem] * 3 + [any_space] * 6,
        out_specs=vmem,
        scratch_shapes=[
            pltpu.VMEM((packets, chunks, rows, width), bf16),
            pltpu.VMEM((stages, chunks, block, width), bf16),
            pltpu.VMEM((depth, all_width), bf16),
            pltpu.VMEM((chunks, q_width, width), bf16),
            pltpu.VMEM(cache_keys.shape, bf16),
            pltpu.VMEM(cache_values.shape, bf16),
            pltpu.VMEM((rows, all_width), f32),
            pltpu.VMEM((packets, rows, all_width), bf16),
            pltpu.VMEM((packets, rows, q_width), bf16),
            pltpu.VMEM((stages, q_heads, rows, HD), bf16),
            pltpu.VMEM((packets, rows, q_width), bf16),
            pltpu.VMEM((steps, n // 2, block, width), bf16),
            pltpu.VMEM((steps, n // 2, block, width), bf16),
            pltpu.VMEM((steps, n // 2, block, width), bf16),
            pltpu.VMEM((steps, block, width), bf16),
            pltpu.VMEM((steps, block, width), bf16),
            pltpu.VMEM((steps, 2, block, width), bf16),
            pltpu.VMEM((steps, 2, block, width), bf16),
            dma((5 + chunks,)),
            dma((2, chunks)),
            dma((2, stages, chunks)),
            dma((2, 7, steps)),
            dma((2, q_heads)),
            dma((2, stages, q_heads)),
            dma((2, 4, steps)),
        ],
        compiler_params=pltpu.CompilerParams(
            collective_id=0, has_side_effects=True, vmem_limit_bytes=VMEM_LIMIT
        ),
        name="layer",
    )(flags, lengths, x, cosine, sine, wq, wk, wv, wo, cache_keys, cache_values)


def local(
    hidden_rows, norm_gain, w_query, w_key, w_value, w_out, cache_keys, cache_values,
    slot_of_request, span_length, prefix_length,
):
    per_device = hidden_rows.shape[1]
    data_index = lax.axis_index("dp")
    span_rows = hidden_rows.shape[0] * lax.axis_size("tensor")
    stages = lax.axis_size("dp").bit_length() - 1
    ids = jnp.arange(per_device, dtype=jnp.int32) + data_index * per_device
    requests = jnp.arange(slot_of_request.shape[0], dtype=jnp.int32)
    mine = jnp.sum(jnp.where(requests[None, :] == ids[:, None], slot_of_request[None, :], 0), axis=1)
    masks = jnp.bitwise_xor(mine // per_device, data_index)
    flip = masks[0] != 1
    mask = jnp.where(flip, masks[0], masks[1])
    match = slot_of_request[None, :] == ids[:, None]
    request_of = jnp.sum(jnp.where(match, requests[None, :], 0), axis=1)
    slot_prefix = jnp.sum(jnp.where(match, prefix_length[None, :], 0), axis=1)
    slot_span = jnp.sum(jnp.where(match, span_length[None, :], 0), axis=1)
    swapped = jnp.bitwise_xor(request_of[0] // per_device, data_index) != 1
    prefix = jnp.where(swapped, slot_prefix[::-1], slot_prefix)
    span = jnp.where(swapped, slot_span[::-1], slot_span)
    bits = (mask // 2 ** (stages - 1 - jnp.arange(stages, dtype=jnp.int32))) % 2
    flags = jnp.concatenate([bits, swapped.astype(jnp.int32)[None]]).astype(jnp.float32)
    lengths = jnp.concatenate([prefix, span])

    floats = hidden_rows.astype(jnp.float32)
    normed = (
        floats * lax.rsqrt(jnp.mean(floats * floats, axis=-1, keepdims=True) + norm_eps) * norm_gain
    ).astype(jnp.bfloat16)
    normed = jnp.transpose(jnp.where(flip, normed[:, ::-1], normed), (1, 0, 2))

    frequency = rope_base ** (-(jnp.arange(HD // 2, dtype=jnp.float32) * 2.0 / HD))
    positions = (prefix[:, None] + jnp.arange(span_rows, dtype=jnp.int32)[None, :]).astype(
        jnp.float32
    )
    angles = positions[:, :, None] * frequency
    cosine, sine = jnp.cos(angles), jnp.sin(angles)
    cosine = jnp.concatenate([cosine, cosine], axis=-1)
    sine = jnp.concatenate([-sine, sine], axis=-1)
    result = layer(
        flags, lengths, normed, cosine, sine, w_query, w_key, w_value, w_out,
        cache_keys, cache_values,
    )
    return jnp.transpose(jnp.where(flip, result[::-1], result), (1, 0, 2))


def solution(mesh):
    placed = (
        P("tensor", "dp", None),
        P(),
        P(None, "tensor"),
        P(None, "tensor"),
        P(None, "tensor"),
        P("tensor", None),
        P("dp", None, "tensor"),
        P("dp", None, "tensor"),
        P(),
        P(),
        P(),
    )
    return jax.shard_map(
        local, mesh=mesh, in_specs=placed, out_specs=P("tensor", "dp", None), check_vma=False
    )
```

```python
import functools

import jax
import jax.numpy as jnp
import numpy as np
from jax import lax
from jax.experimental import pallas as pl
from jax.experimental.pallas import tpu as pltpu
from jax.sharding import PartitionSpec as P

HD = 128
rope_base = 500000.0
norm_eps = 1e-05
masked = -1e30
log2e = 1.4426950408889634
VMEM_LIMIT = 62 << 20
MESH = pl.DeviceIdType.MESH


def peers():
    n = lax.axis_size("tensor")
    t = lax.axis_index("tensor")
    core = lax.rem(t, 2)
    return t, core, lax.rem(t + 2, n), lax.rem(t + n - 2, n), t + 1 - 2 * core


def greet(devices):
    barrier = pltpu.get_barrier_semaphore()
    for device in devices:
        pl.semaphore_signal(barrier, inc=1, device_id=device, device_id_type=MESH)
    pl.semaphore_wait(barrier, len(devices))


def remote(source, target, sems, index, device):
    return pltpu.make_async_remote_copy(
        src_ref=source,
        dst_ref=target,
        send_sem=sems.at[(0, *index)],
        recv_sem=sems.at[(1, *index)],
        device_id=device,
        device_id_type=MESH,
    )


TO_RIGHT, TO_LEFT, TO_SIB, ONWARD, SIB_LEFT, SIB_RIGHT, SIB_FAR = range(7)
SWAP, FAR, SUM_RIGHT, SUM_LEFT = range(4)
NEIGHBOURS, FAR_BLOCK, PRODUCT = 2, 4, 5
CHIP_SUM, PASS_ON, RESULT = 1, 3, 5
ROWS_FIRST, ROWS_SECOND = 3, 7
HEAD_FIRST, HEAD_SECOND = 2, 4


def layer_kernel(
    plan, flags_ref, lengths_ref, x_ref, cos_ref, sin_ref, frequency_ref,
    wq_ref, wk_ref, wv_ref, wo_ref, ck_ref, cv_ref, out_ref,
    rows, ordered, hop, hopped, weights, weights_out, cache_k, cache_v, total, packed, heads,
    back, backed, home, mine, swap_out, swap_in, far_out, far_in, sum_out, sum_in,
    local_sem, near_sem, hop_sem, gather_sem, near_back_sem, back_sem, reduce_sem,
):
    chunks, stage_bits, q_heads = plan
    t, core, right, left, sib = peers()
    n = lax.axis_size("tensor")
    chips = n // 2
    far = lax.rem(t + chips, n)
    z = t // 2
    z_right, z_left, z_far = right // 2, left // 2, far // 2
    d = lax.axis_index("dp")
    block = x_ref.shape[1]
    span_rows = block * n
    width = rows.shape[-1]
    q_width, kv_width = wq_ref.shape[1], wk_ref.shape[1]
    bf16, f32 = jnp.bfloat16, jnp.float32
    total_chunks = 2 * chunks

    def flipped(mask):
        other = d
        for bit in range(mask.bit_length()):
            size = 1 << bit
            if mask & size:
                other = other + size - 2 * size * lax.rem(d // size, 2)
        return {"dp": other}

    def across(device):
        return {"tensor": device}

    stage_masks = (
        [i << stage_bits[1] for i in range(1, 1 << stage_bits[0])],
        list(range(1, 1 << stage_bits[1])),
    )

    def at(device):
        return pl.ds(pl.multiple_of(device * block, block), block)

    def columns(k):
        return pl.ds(pl.multiple_of(k * width, width), width)

    def head_columns(h):
        return pl.ds(pl.multiple_of(h * HD, HD), HD)

    def near(k):
        return remote(
            ordered.at[0, k], rows.at[0, k, at(t), :], near_sem, (k,), flipped(1)
        )

    def hop_source(s, k):
        return ordered.at[1, k] if s == 0 else hopped.at[k]

    def hops(s, i, k):
        return remote(
            hop_source(s, k), hop.at[s, i, k], hop_sem, (s, i, k), flipped(stage_masks[s][i])
        )

    def gather(kind, q, owner, device):
        view = rows.at[q // chunks, lax.rem(q, chunks), at(owner), :]
        return remote(view, view, gather_sem, (kind, q), across(device))

    def onward(q):
        odd = lax.rem(q, 2)
        return gather(
            ONWARD, q, left * (1 - odd) + right * odd, right * (1 - odd) + left * odd
        )

    def near_back(h):
        return remote(
            heads.at[0, :, head_columns(h)], home.at[0, :, head_columns(h)],
            near_back_sem, (h,), flipped(1),
        )

    def back_source(s, h):
        return heads.at[1, :, head_columns(h)] if s == 0 else backed.at[h]

    def backs(s, i, h):
        return remote(
            back_source(s, h), back.at[s, i, h], back_sem, (s, i, h), flipped(stage_masks[s][i])
        )

    def swap(r):
        return remote(swap_out.at[r], swap_in.at[r], reduce_sem, (SWAP, r), across(sib))

    def far_sum(r):
        odd = lax.rem(r, 2)
        return remote(
            far_out.at[r], far_in.at[r], reduce_sem, (FAR, r),
            across(right * (1 - odd) + left * odd),
        )

    def sum_right(r):
        return remote(
            sum_out.at[r, 0], sum_in.at[r, 0], reduce_sem, (SUM_RIGHT, r), across(right)
        )

    def sum_left(r):
        return remote(
            sum_out.at[r, 1], sum_in.at[r, 1], reduce_sem, (SUM_LEFT, r), across(left)
        )

    def weight_copy(index):
        ref = (wq_ref, wk_ref, wv_ref)[index]
        start = (0, q_width, q_width + kv_width)[index]
        return pltpu.make_async_copy(
            ref, weights.at[:, pl.ds(start, ref.shape[1])], local_sem.at[index]
        )

    def out_copy(j):
        return pltpu.make_async_copy(
            wo_ref.at[:, columns(j)], weights_out.at[j], local_sem.at[5 + j]
        )

    cache_copies = (
        pltpu.make_async_copy(ck_ref, cache_k, local_sem.at[3]),
        pltpu.make_async_copy(cv_ref, cache_v, local_sem.at[4]),
    )

    greet(
        [across(right), across(left), across(sib)]
        + [flipped(m) for masks in stage_masks for m in masks]
    )

    def flip_flags():
        return flags_ref[0], 1.0 - flags_ref[0]

    def swap_flags():
        return flags_ref[1], 1.0 - flags_ref[1]

    def keep(s):
        first = 2 + s * (1 << stage_bits[0])
        return tuple(flags_ref[first + i] for i in range(1 << stage_bits[s]))

    def mix(parts, flags):
        value = parts[0].astype(f32) * flags[0]
        for part, flag in zip(parts[1:], flags[1:]):
            value = value + part.astype(f32) * flag
        return value.astype(bf16)

    def order_rows(k, carry):
        first, second = x_ref[0, :, columns(k)], x_ref[1, :, columns(k)]
        ordered[0, k] = mix((second, first), flip_flags())
        near(k).start()
        ordered[1, k] = mix((first, second), flip_flags())
        for i in range(len(stage_masks[0])):
            hops(0, i, k).start()
        return carry

    lax.fori_loop(0, chunks, order_rows, 0)
    for index in range(3):
        weight_copy(index).start()
    for copy in cache_copies:
        copy.start()
    for j in range(chunks):
        out_copy(j).start()
    total[...] = jnp.zeros_like(total)

    sib_of = 1 - 2 * core
    attend_near = chunks + PRODUCT
    attend_other = total_chunks + PRODUCT
    reduce_near = attend_near + q_heads + 1
    reduce_other = max(attend_other + q_heads + HEAD_SECOND, reduce_near + chunks)
    last = reduce_other + chunks + RESULT
    contract = (((1,), (1,)), ((), ()))

    def within(value, low, high):
        return (value >= low) & (value < high)

    def reduce_index(tick):
        first = tick - reduce_near
        second = tick - reduce_other
        on_first, on_second = within(first, 0, chunks), within(second, 0, chunks)
        late = lax.select(second >= 0, 1, 0)
        return first * (1 - late) + (second + chunks) * late, on_first | on_second

    def tick_body(tick, carry):
        @pl.when(tick < chunks)
        def _():
            near(tick).wait_recv()

        @pl.when(tick < total_chunks)
        def _():
            gather(TO_RIGHT, tick, t, right).start()
            gather(TO_LEFT, tick, t, left).start()
            gather(TO_SIB, tick, t, sib).start()

        @pl.when(within(tick - NEIGHBOURS, 0, total_chunks))
        def _():
            q = tick - NEIGHBOURS
            gather(TO_RIGHT, q, left, right).wait_recv()
            gather(TO_LEFT, q, right, left).wait_recv()
            onward(q).start()
            gather(SIB_LEFT, q, left, sib).start()
            gather(SIB_RIGHT, q, right, sib).start()

        @pl.when(within(tick - FAR_BLOCK, 0, total_chunks))
        def _():
            q = tick - FAR_BLOCK
            onward(q).wait_recv()
            gather(SIB_FAR, q, far, sib).start()

        for s, lag in enumerate((ROWS_FIRST, ROWS_SECOND)):

            @pl.when(within(tick - lag, 0, chunks))
            def _(s=s, k=tick - lag):
                found = [hop_source(s, k)[...]]
                for i in range(len(stage_masks[s])):
                    hops(s, i, k).wait_recv()
                    found.append(hop[s, i, k])
                value = mix(found, keep(s))
                if s == 0:
                    hopped[k] = value
                    for i in range(len(stage_masks[1])):
                        hops(1, i, k).start()
                else:
                    rows[1, k, at(t), :] = value

        @pl.when(tick == PRODUCT - 1)
        def _():
            for copy in cache_copies:
                copy.wait()
            for cache in (cache_k, cache_v):
                first, second = cache[0], cache[1]
                cache[0] = mix((second, first), swap_flags())
                cache[1] = mix((first, second), swap_flags())
            for index in range(3):
                weight_copy(index).wait()

        r, on = reduce_index(tick - PASS_ON)

        @pl.when(on)
        def _():
            odd = lax.rem(r, 2).astype(f32)
            far_sum(r).wait_recv()
            passed = far_in[r].astype(f32)
            sum_out[r, 0] = (mine[r, z_right].astype(f32) + passed * (1.0 - odd)).astype(bf16)
            sum_out[r, 1] = (mine[r, z_left].astype(f32) + passed * odd).astype(bf16)
            sum_right(r).start()
            sum_left(r).start()

        r, on = reduce_index(tick - CHIP_SUM)

        @pl.when(on)
        def _():
            swap(r).wait_recv()
            value = mine[r].astype(f32) + swap_in[r].astype(f32)
            mine[r] = value.astype(bf16)
            far_out[r] = mine[r, z_far]
            far_sum(r).start()

        r, on = reduce_index(tick)

        @pl.when(on)
        def _():
            p, j = r // chunks, lax.rem(r, chunks)

            @pl.when(r == 0)
            def _():
                for h in range(q_heads):
                    near_back(h).wait_recv()

            @pl.when(r < chunks)
            def _():
                out_copy(j).wait()

            part = jnp.dot(home[p], weights_out[j], preferred_element_type=f32)
            part = part.reshape(chips, 2, block, width)
            mine[r] = jnp.where(core == 0, part[:, 0], part[:, 1]).astype(bf16)
            swap_out[r] = jnp.where(core == 0, part[:, 1], part[:, 0]).astype(bf16)
            swap(r).start()

        @pl.when(within(tick - PRODUCT, 0, total_chunks))
        def _():
            q = tick - PRODUCT
            p, k = q // chunks, lax.rem(q, chunks)
            gather(TO_SIB, q, sib, sib).wait_recv()
            gather(SIB_LEFT, q, left + sib_of, sib).wait_recv()
            gather(SIB_RIGHT, q, right + sib_of, sib).wait_recv()
            gather(SIB_FAR, q, far + sib_of, sib).wait_recv()
            total[...] += jnp.dot(rows[p, k], weights[columns(k), :], preferred_element_type=f32)

            @pl.when(k == chunks - 1)
            def _():
                prefix = lengths_ref[p]
                angle = frequency_ref[...] * prefix.astype(f32)
                base_cos, base_sin = jnp.cos(angle)[0:1], jnp.sin(angle)[0:1]
                cosine = cos_ref[...] * base_cos - sin_ref[...] * base_sin
                sine = sin_ref[...] * base_cos + cos_ref[...] * base_sin
                lane = lax.broadcasted_iota(jnp.int32, sine.shape, 1)
                sine = jnp.where(lane < HD // 2, -sine, sine)
                for h in range((q_width + kv_width) // HD):
                    place = pl.ds(h * HD, HD)
                    value = total[:, place]
                    value = value * cosine + pltpu.roll(value, HD // 2, axis=1) * sine
                    if h < q_heads:
                        value = value * (HD ** (-0.5) * log2e)
                    packed[p, :, place] = value.astype(bf16)
                place = pl.ds(q_width + kv_width, kv_width)
                packed[p, :, place] = total[:, place].astype(bf16)
                total[...] = jnp.zeros_like(total)

        @pl.when(
            within(tick - attend_near, 0, q_heads) | within(tick - attend_other, 0, q_heads)
        )
        def _():
            late = lax.select(tick >= attend_other, 1, 0)
            p = late
            h = tick - attend_near * (1 - late) - attend_other * late
            prefix, span = lengths_ref[p], lengths_ref[2 + p]
            prefix_rows = cache_k.shape[1]
            keys_new = packed[p, :, pl.ds(q_width, kv_width)]
            values_new = packed[p, :, pl.ds(q_width + kv_width, kv_width)]
            old_column = lax.broadcasted_iota(jnp.int32, (1, prefix_rows), 1)
            old_bias = jnp.where(old_column < prefix, 0.0, masked)
            row = lax.broadcasted_iota(jnp.int32, (span_rows, span_rows), 0)
            column = lax.broadcasted_iota(jnp.int32, (span_rows, span_rows), 1)
            new_bias = jnp.where((column <= row) & (column < span), 0.0, masked)
            query = packed[p, :, head_columns(h)]
            old = lax.dot_general(query, cache_k[p], contract, preferred_element_type=f32)
            old = old + old_bias
            new = lax.dot_general(query, keys_new, contract, preferred_element_type=f32)
            new = new + new_bias
            top = jnp.maximum(
                jnp.max(old, axis=1, keepdims=True), jnp.max(new, axis=1, keepdims=True)
            )
            old = jnp.exp2(old - top)
            new = jnp.exp2(new - top)
            weight_sum = jnp.sum(old, axis=1, keepdims=True) + jnp.sum(
                new, axis=1, keepdims=True
            )
            mixed = jnp.dot(old.astype(bf16), cache_v[p], preferred_element_type=f32)
            mixed += jnp.dot(new.astype(bf16), values_new, preferred_element_type=f32)
            heads[p, :, head_columns(h)] = (mixed / weight_sum).astype(bf16)

            @pl.when(p == 0)
            def _():
                near_back(h).start()

            @pl.when(p == 1)
            def _():
                for i in range(len(stage_masks[0])):
                    backs(0, i, h).start()

        for s, lag in enumerate((HEAD_FIRST, HEAD_SECOND)):

            @pl.when(within(tick - attend_other - lag, 0, q_heads))
            def _(s=s, h=tick - attend_other - lag):
                found = [back_source(s, h)[...]]
                for i in range(len(stage_masks[s])):
                    backs(s, i, h).wait_recv()
                    found.append(back[s, i, h])
                value = mix(found, keep(s))
                if s == 0:
                    backed[h] = value
                    for i in range(len(stage_masks[1])):
                        backs(1, i, h).start()
                else:
                    home[1, :, head_columns(h)] = value

        r, on = reduce_index(tick - RESULT)

        @pl.when(on)
        def _():
            p, j = r // chunks, lax.rem(r, chunks)
            sum_right(r).wait_recv()
            sum_left(r).wait_recv()
            value = (
                mine[r, z].astype(f32) + sum_in[r, 0].astype(f32) + sum_in[r, 1].astype(f32)
            ).astype(bf16)

            @pl.when(p == 0)
            def _():
                out_ref[0, :, columns(j)] = value

            @pl.when(p == 1)
            def _():
                first = out_ref[0, :, columns(j)]
                out_ref[0, :, columns(j)] = mix((value, first), flip_flags())
                out_ref[1, :, columns(j)] = mix((first, value), flip_flags())

        return carry

    lax.fori_loop(0, last, tick_body, 0)

    def drain_rows(k, carry):
        near(k).wait_send()
        for s in range(2):
            for i in range(len(stage_masks[s])):
                hops(s, i, k).wait_send()
        return carry

    def drain_blocks(q, carry):
        gather(TO_RIGHT, q, t, right).wait_send()
        gather(TO_LEFT, q, t, left).wait_send()
        gather(TO_SIB, q, t, sib).wait_send()
        onward(q).wait_send()
        gather(SIB_LEFT, q, left, sib).wait_send()
        gather(SIB_RIGHT, q, right, sib).wait_send()
        gather(SIB_FAR, q, far, sib).wait_send()
        swap(q).wait_send()
        far_sum(q).wait_send()
        sum_right(q).wait_send()
        sum_left(q).wait_send()
        return carry

    def drain_heads(h, carry):
        near_back(h).wait_send()
        for s in range(2):
            for i in range(len(stage_masks[s])):
                backs(s, i, h).wait_send()
        return carry

    lax.fori_loop(0, chunks, drain_rows, 0)
    lax.fori_loop(0, total_chunks, drain_blocks, 0)
    lax.fori_loop(0, q_heads, drain_heads, 0)


def layer(flags, lengths, x, cosine, sine, frequency, wq, wk, wv, wo, cache_keys, cache_values, chunks=8):
    packets, block, depth = x.shape
    n, dp = lax.axis_size("tensor"), lax.axis_size("dp")
    low_bits = (dp.bit_length() - 1) // 2
    stage_bits = (dp.bit_length() - 1 - low_bits, low_bits)
    most = max((1 << b) - 1 for b in stage_bits)
    q_width, kv_width = wq.shape[1], wk.shape[1]
    all_width = q_width + 2 * kv_width
    q_heads = q_width // HD
    rows, width = block * n, depth // chunks
    bf16, f32 = jnp.bfloat16, jnp.float32
    any_space = pl.BlockSpec(memory_space=pl.ANY)
    smem = pl.BlockSpec(memory_space=pltpu.SMEM)
    vmem = pl.BlockSpec(memory_space=pltpu.VMEM)
    steps = packets * chunks
    dma = pltpu.SemaphoreType.DMA
    return pl.pallas_call(
        functools.partial(layer_kernel, (chunks, stage_bits, q_heads)),
        out_shape=jax.ShapeDtypeStruct((packets, block, depth), bf16),
        in_specs=[smem] * 2 + [vmem] * 4 + [any_space] * 6,
        out_specs=vmem,
        scratch_shapes=[
            pltpu.VMEM((packets, chunks, rows, width), bf16),
            pltpu.VMEM((packets, chunks, block, width), bf16),
            pltpu.VMEM((2, most, chunks, block, width), bf16),
            pltpu.VMEM((chunks, block, width), bf16),
            pltpu.VMEM((depth, all_width), bf16),
            pltpu.VMEM((chunks, q_width, width), bf16),
            pltpu.VMEM(cache_keys.shape, bf16),
            pltpu.VMEM(cache_values.shape, bf16),
            pltpu.VMEM((rows, all_width), f32),
            pltpu.VMEM((packets, rows, all_width), bf16),
            pltpu.VMEM((packets, rows, q_width), bf16),
            pltpu.VMEM((2, most, q_heads, rows, HD), bf16),
            pltpu.VMEM((q_heads, rows, HD), bf16),
            pltpu.VMEM((packets, rows, q_width), bf16),
            pltpu.VMEM((steps, n // 2, block, width), bf16),
            pltpu.VMEM((steps, n // 2, block, width), bf16),
            pltpu.VMEM((steps, n // 2, block, width), bf16),
            pltpu.VMEM((steps, block, width), bf16),
            pltpu.VMEM((steps, block, width), bf16),
            pltpu.VMEM((steps, 2, block, width), bf16),
            pltpu.VMEM((steps, 2, block, width), bf16),
            dma((5 + chunks,)),
            dma((2, chunks)),
            dma((2, 2, most, chunks)),
            dma((2, 7, steps)),
            dma((2, q_heads)),
            dma((2, 2, most, q_heads)),
            dma((2, 4, steps)),
        ],
        compiler_params=pltpu.CompilerParams(
            collective_id=0, has_side_effects=True, vmem_limit_bytes=VMEM_LIMIT
        ),
        name="layer",
    )(flags, lengths, x, cosine, sine, frequency, wq, wk, wv, wo, cache_keys, cache_values)


def local(
    hidden_rows, norm_gain, w_query, w_key, w_value, w_out, cache_keys, cache_values,
    slot_of_request, span_length, prefix_length,
):
    span_rows = hidden_rows.shape[0] * lax.axis_size("tensor")
    per_device = hidden_rows.shape[1]
    data_index = lax.axis_index("dp")
    low = 1 << ((lax.axis_size("dp").bit_length() - 1) // 2)
    high = lax.axis_size("dp") // low
    ids = jnp.arange(per_device, dtype=jnp.int32) + data_index * per_device
    requests = jnp.arange(slot_of_request.shape[0], dtype=jnp.int32)
    mine = requests[None, :] == ids[:, None]
    masks = jnp.bitwise_xor(
        jnp.sum(jnp.where(mine, slot_of_request[None, :], 0), axis=1) // per_device, data_index
    )
    flip = masks[0] != 1
    mask = jnp.where(flip, masks[0], masks[1])
    match = slot_of_request[None, :] == ids[:, None]
    near = jnp.bitwise_xor(requests // per_device, data_index) == 1
    swapped = ~jnp.any(match[0] & near)
    packet = jnp.stack([jnp.where(swapped, match[1], match[0]), jnp.where(swapped, match[0], match[1])])
    lengths = jnp.sum(
        jnp.where(packet[None], jnp.stack([prefix_length, span_length])[:, None, :], 0), axis=-1
    ).reshape(-1)
    flags = jnp.concatenate(
        [
            flip[None], swapped[None],
            mask // low == jnp.arange(high, dtype=jnp.int32),
            mask % low == jnp.arange(low, dtype=jnp.int32),
        ]
    ).astype(jnp.float32)
    floats = hidden_rows.astype(jnp.float32)
    normed = (
        floats * lax.rsqrt(jnp.mean(floats * floats, axis=-1, keepdims=True) + norm_eps) * norm_gain
    ).astype(jnp.bfloat16)
    half = rope_base ** (-(np.arange(HD // 2, dtype=np.float64) * 2.0 / HD))
    frequency = np.concatenate([half, half])
    angles = np.arange(span_rows, dtype=np.float64)[:, None] * frequency
    result = layer(
        flags, lengths, jnp.transpose(normed, (1, 0, 2)),
        jnp.asarray(np.cos(angles), jnp.float32), jnp.asarray(np.sin(angles), jnp.float32),
        jnp.asarray(np.broadcast_to(frequency, (8, HD)), jnp.float32),
        w_query, w_key, w_value, w_out, cache_keys, cache_values,
    )
    return jnp.transpose(result, (1, 0, 2))


def solution(mesh):
    placed = (
        P("tensor", "dp", None),
        P(),
        P(None, "tensor"),
        P(None, "tensor"),
        P(None, "tensor"),
        P("tensor", None),
        P("dp", None, "tensor"),
        P("dp", None, "tensor"),
        P(),
        P(),
        P(),
    )
    return jax.shard_map(
        local, mesh=mesh, in_specs=placed, out_specs=P("tensor", "dp", None), check_vma=False
    )
```

```python
import functools

import jax
import jax.numpy as jnp
import numpy as np
from jax import lax
from jax.experimental import pallas as pl
from jax.experimental.pallas import tpu as pltpu
from jax.sharding import PartitionSpec as P

HD = 128
rope_base = 500000.0
norm_eps = 1e-05
masked = -1e30
log2e = 1.4426950408889634
VMEM_LIMIT = 49 << 20
MESH = pl.DeviceIdType.MESH


def peers():
    n = lax.axis_size("tensor")
    t = lax.axis_index("tensor")
    core = lax.rem(t, 2)
    return t, core, lax.rem(t + 2, n), lax.rem(t + n - 2, n), t + 1 - 2 * core


def greet(devices):
    barrier = pltpu.get_barrier_semaphore()
    for device in devices:
        pl.semaphore_signal(barrier, inc=1, device_id=device, device_id_type=MESH)


def await_greetings(devices):
    pl.semaphore_wait(pltpu.get_barrier_semaphore(), len(devices))


def remote(source, target, sems, index, device):
    return pltpu.make_async_remote_copy(
        src_ref=source,
        dst_ref=target,
        send_sem=sems.at[(0, *index)],
        recv_sem=sems.at[(1, *index)],
        device_id=device,
        device_id_type=MESH,
    )


TO_RIGHT, TO_LEFT, TO_SIB, ONWARD, SIB_LEFT, SIB_RIGHT, SIB_FAR = range(7)
FLIP, SWAPPED, PREFIX, SPAN, KEEP = 0, 1, 2, 4, 6
SWAP, FAR, SUM_RIGHT, SUM_LEFT = range(4)
NEIGHBOURS, FAR_BLOCK, PRODUCT = 1, 2, 3
CHIP_SUM, PASS_ON, RESULT = 1, 3, 5
ROWS_FIRST, ROWS_SECOND = 1, 3
HEAD_FIRST, HEAD_SECOND = 2, 4
GROUP = 1
REDUCE_LAG = 1


def table_kernel(bits, slot_ref, prefix_ref, span_ref, table_ref):
    d = lax.axis_index("dp")
    mask_0 = lax.bitwise_xor(slot_ref[2 * d] // 2, d)
    mask_1 = lax.bitwise_xor(slot_ref[2 * d + 1] // 2, d)
    flip = lax.select(mask_0 != 1, 1, 0)
    mask = mask_0 * flip + mask_1 * (1 - flip)
    table_ref[FLIP] = flip
    low = 1 << bits[1]
    place = KEEP
    for part, count in zip((mask // low, lax.rem(mask, low)), bits):
        for i in range(1 << count):
            table_ref[place] = lax.select(part == i, 1, 0)
            place += 1

    def look_up(i, carry):
        request, prefix_0, prefix_1, span_0, span_1 = carry
        is_0 = lax.select(slot_ref[i] == 2 * d, 1, 0)
        is_1 = lax.select(slot_ref[i] == 2 * d + 1, 1, 0)
        return (
            request + i * is_0,
            prefix_0 + prefix_ref[i] * is_0,
            prefix_1 + prefix_ref[i] * is_1,
            span_0 + span_ref[i] * is_0,
            span_1 + span_ref[i] * is_1,
        )

    request, prefix_0, prefix_1, span_0, span_1 = lax.fori_loop(
        0, slot_ref.shape[0], look_up, (jnp.int32(0),) * 5
    )
    swapped = lax.select(lax.bitwise_xor(request // 2, d) != 1, 1, 0)
    table_ref[SWAPPED] = swapped
    table_ref[PREFIX] = prefix_1 * swapped + prefix_0 * (1 - swapped)
    table_ref[PREFIX + 1] = prefix_0 * swapped + prefix_1 * (1 - swapped)
    table_ref[SPAN] = span_1 * swapped + span_0 * (1 - swapped)
    table_ref[SPAN + 1] = span_0 * swapped + span_1 * (1 - swapped)


def dp_stage_bits():
    bits = lax.axis_size("dp").bit_length() - 1
    return bits - bits // 2, bits // 2


def requests_table(slots, prefix, span):
    bits = dp_stage_bits()
    smem = pl.BlockSpec(memory_space=pltpu.SMEM)
    return pl.pallas_call(
        functools.partial(table_kernel, bits),
        out_shape=jax.ShapeDtypeStruct((KEEP + sum(1 << b for b in bits),), jnp.int32),
        in_specs=[smem] * 3,
        out_specs=smem,
        name="requests_table",
    )(slots, prefix, span)


def layer_kernel(
    plan, table_ref, x_ref, cos_ref, sin_ref, frequency_ref,
    wq_ref, wk_ref, wv_ref, wo_ref, ck_ref, cv_ref, out_ref,
    rows, ordered, hop, hopped, weights, weights_out, cache_k, cache_v, total, packed, heads,
    back, backed, home, swap_in, far_in, sum_in,
    local_sem, near_sem, hop_sem, gather_sem, near_back_sem, back_sem, reduce_sem,
):
    chunks, stage_bits, q_heads = plan
    t, core, right, left, sib = peers()
    n = lax.axis_size("tensor")
    chips = n // 2
    far = lax.rem(t + chips, n)
    z = t // 2
    z_right, z_left, z_far = right // 2, left // 2, far // 2
    d = lax.axis_index("dp")
    block = x_ref.shape[1]
    span_rows = block * n
    width = rows.shape[-1]
    q_width, kv_width = wq_ref.shape[1], wk_ref.shape[1]
    bf16, f32 = jnp.bfloat16, jnp.float32
    total_chunks = 2 * chunks

    def flipped(mask):
        other = d
        for bit in range(mask.bit_length()):
            size = 1 << bit
            if mask & size:
                other = other + size - 2 * size * lax.rem(d // size, 2)
        return {"dp": other}

    def across(device):
        return {"tensor": device}

    stage_masks = (
        [i << stage_bits[1] for i in range(1, 1 << stage_bits[0])],
        list(range(1, 1 << stage_bits[1])),
    )

    def at(device):
        return pl.ds(pl.multiple_of(device * block, block), block)

    def columns(k):
        return pl.ds(pl.multiple_of(k * width, width), width)

    groups = q_heads // GROUP

    def head_columns(h):
        return pl.ds(pl.multiple_of(h * HD, HD), HD)

    def group_columns(g):
        return pl.ds(pl.multiple_of(g * GROUP * HD, GROUP * HD), GROUP * HD)

    def near(k):
        return remote(
            ordered.at[0, k], rows.at[0, k, at(t), :], near_sem, (k,), flipped(1)
        )

    def hop_source(s, k):
        return ordered.at[1, k] if s == 0 else hopped.at[k]

    def hops(s, i, k):
        return remote(
            hop_source(s, k), hop.at[s, i, k], hop_sem, (s, i, k), flipped(stage_masks[s][i])
        )

    def gather(kind, q, owner, device):
        view = rows.at[q // chunks, lax.rem(q, chunks), at(owner), :]
        return remote(view, view, gather_sem, (kind, q), across(device))

    def onward(q):
        odd = lax.rem(q, 2)
        return gather(
            ONWARD, q, left * (1 - odd) + right * odd, right * (1 - odd) + left * odd
        )

    def near_back(h):
        return remote(
            heads.at[0, :, group_columns(h)], home.at[0, :, group_columns(h)],
            near_back_sem, (h,), flipped(1),
        )

    def back_source(s, h):
        return heads.at[1, :, group_columns(h)] if s == 0 else backed.at[h]

    def backs(s, i, h):
        return remote(
            back_source(s, h), back.at[s, i, h], back_sem, (s, i, h), flipped(stage_masks[s][i])
        )

    def kept(r, place):
        return rows.at[r // chunks, lax.rem(r, chunks), place, :]

    def swap(r):
        return remote(
            kept(r, pl.ds(span_rows // 2, span_rows // 2)), swap_in.at[r],
            reduce_sem, (SWAP, r), across(sib),
        )

    def far_sum(r):
        odd = lax.rem(r, 2)
        return remote(
            kept(r, at(z_far)), far_in.at[r], reduce_sem, (FAR, r),
            across(right * (1 - odd) + left * odd),
        )

    def sum_right(r):
        return remote(
            swap_in.at[r, pl.ds(0, block)], sum_in.at[r, 0], reduce_sem, (SUM_RIGHT, r), across(right)
        )

    def sum_left(r):
        return remote(
            swap_in.at[r, pl.ds(block, block)], sum_in.at[r, 1], reduce_sem, (SUM_LEFT, r), across(left)
        )

    def weight_copy(index):
        ref = (wq_ref, wk_ref, wv_ref)[index]
        start = (0, q_width, q_width + kv_width)[index]
        return pltpu.make_async_copy(
            ref, weights.at[:, pl.ds(start, ref.shape[1])], local_sem.at[index]
        )

    def out_copy(j):
        return pltpu.make_async_copy(
            wo_ref.at[:, columns(j)], weights_out.at[j], local_sem.at[5 + j]
        )

    cache_copies = (
        pltpu.make_async_copy(ck_ref, cache_k, local_sem.at[3]),
        pltpu.make_async_copy(cv_ref, cache_v, local_sem.at[4]),
    )

    devices = [across(right), across(left), across(sib)]
    devices += [flipped(m) for masks in stage_masks for m in masks]
    greet(devices)

    def flag(index):
        return table_ref[index].astype(f32)

    def flip_flags():
        return flag(FLIP), 1.0 - flag(FLIP)

    def swap_flags():
        return flag(SWAPPED), 1.0 - flag(SWAPPED)

    def keep(s):
        first = KEEP + s * (1 << stage_bits[0])
        return tuple(flag(first + i) for i in range(1 << stage_bits[s]))

    def mix(parts, flags):
        value = parts[0].astype(f32) * flags[0]
        for part, flag in zip(parts[1:], flags[1:]):
            value = value + part.astype(f32) * flag
        return value.astype(bf16)

    for copy in cache_copies:
        copy.start()

    def order_rows(k, carry):
        first, second = x_ref[0, :, columns(k)], x_ref[1, :, columns(k)]
        ordered[0, k] = mix((second, first), flip_flags())
        ordered[1, k] = mix((first, second), flip_flags())
        return carry

    lax.fori_loop(0, chunks, order_rows, 0)
    total[...] = jnp.zeros_like(total)
    await_greetings(devices)

    def send_rows(k, carry):
        near(k).start()
        for i in range(len(stage_masks[0])):
            hops(0, i, k).start()
        return carry

    lax.fori_loop(0, chunks, send_rows, 0)
    for index in range(3):
        weight_copy(index).start()
    for j in range(chunks):
        out_copy(j).start()

    sib_of = 1 - 2 * core
    attend_near = chunks + PRODUCT
    attend_other = total_chunks + PRODUCT
    reduce_near = attend_near + groups + REDUCE_LAG
    reduce_other = max(attend_other + groups + HEAD_SECOND, reduce_near + chunks)
    last = reduce_other + chunks + RESULT
    contract = (((1,), (1,)), ((), ()))

    def within(value, low, high):
        return (value >= low) & (value < high)

    def reduce_index(tick):
        first = tick - reduce_near
        second = tick - reduce_other
        on_first, on_second = within(first, 0, chunks), within(second, 0, chunks)
        late = lax.select(second >= 0, 1, 0)
        return first * (1 - late) + (second + chunks) * late, on_first | on_second

    def tick_body(tick, carry):
        @pl.when(tick < chunks)
        def _():
            near(tick).wait_recv()

        @pl.when(tick < total_chunks)
        def _():
            gather(TO_RIGHT, tick, t, right).start()
            gather(TO_LEFT, tick, t, left).start()
            gather(TO_SIB, tick, t, sib).start()

        @pl.when(within(tick - NEIGHBOURS, 0, total_chunks))
        def _():
            q = tick - NEIGHBOURS
            gather(TO_RIGHT, q, left, right).wait_recv()
            gather(TO_LEFT, q, right, left).wait_recv()
            onward(q).start()
            gather(SIB_LEFT, q, left, sib).start()
            gather(SIB_RIGHT, q, right, sib).start()

        @pl.when(within(tick - FAR_BLOCK, 0, total_chunks))
        def _():
            q = tick - FAR_BLOCK
            onward(q).wait_recv()
            gather(SIB_FAR, q, far, sib).start()

        for s, lag in enumerate((ROWS_FIRST, ROWS_SECOND)):

            @pl.when(within(tick - lag, 0, chunks))
            def _(s=s, k=tick - lag):
                found = [hop_source(s, k)[...]]
                for i in range(len(stage_masks[s])):
                    hops(s, i, k).wait_recv()
                    found.append(hop[s, i, k])
                value = mix(found, keep(s))
                if s == 0:
                    hopped[k] = value
                    for i in range(len(stage_masks[1])):
                        hops(1, i, k).start()
                else:
                    rows[1, k, at(t), :] = value

        @pl.when(tick == PRODUCT - 1)
        def _():
            for copy in cache_copies:
                copy.wait()
            for cache in (cache_k, cache_v):
                first, second = cache[0], cache[1]
                cache[0] = mix((second, first), swap_flags())
                cache[1] = mix((first, second), swap_flags())
            for index in range(3):
                weight_copy(index).wait()

        r, on = reduce_index(tick - PASS_ON)

        @pl.when(on)
        def _():
            odd = lax.rem(r, 2).astype(f32)
            far_sum(r).wait_recv()
            passed = far_in[r].astype(f32)
            swap_in[r, pl.ds(0, block)] = (kept(r, at(z_right))[...].astype(f32) + passed * (1.0 - odd)).astype(bf16)
            swap_in[r, pl.ds(block, block)] = (kept(r, at(z_left))[...].astype(f32) + passed * odd).astype(bf16)
            sum_right(r).start()
            sum_left(r).start()

        r, on = reduce_index(tick - CHIP_SUM)

        @pl.when(on)
        def _():
            swap(r).wait_recv()
            own = kept(r, pl.ds(0, span_rows // 2))
            own[...] = (own[...].astype(f32) + swap_in[r].astype(f32)).astype(bf16)
            far_sum(r).start()

        r, on = reduce_index(tick)

        @pl.when(on)
        def _():
            p, j = r // chunks, lax.rem(r, chunks)

            @pl.when(r == 0)
            def _():
                for g in range(groups):
                    near_back(g).wait_recv()

            @pl.when(r < chunks)
            def _():
                out_copy(j).wait()

            part = jnp.dot(home[p], weights_out[j], preferred_element_type=f32)
            part = part.reshape(chips, 2, block, width)
            gather(TO_RIGHT, r, t, right).wait_send()
            gather(TO_LEFT, r, t, left).wait_send()
            gather(TO_SIB, r, t, sib).wait_send()
            onward(r).wait_send()
            gather(SIB_LEFT, r, left, sib).wait_send()
            gather(SIB_RIGHT, r, right, sib).wait_send()
            gather(SIB_FAR, r, far, sib).wait_send()
            own = jnp.where(core == 0, part[:, 0], part[:, 1]).astype(bf16)
            other = jnp.where(core == 0, part[:, 1], part[:, 0]).astype(bf16)
            kept(r, pl.ds(0, span_rows // 2))[...] = own.reshape(span_rows // 2, width)
            kept(r, pl.ds(span_rows // 2, span_rows // 2))[...] = other.reshape(
                span_rows // 2, width
            )
            swap(r).start()

        @pl.when(within(tick - PRODUCT, 0, total_chunks))
        def _():
            q = tick - PRODUCT
            p, k = q // chunks, lax.rem(q, chunks)
            gather(TO_SIB, q, sib, sib).wait_recv()
            gather(SIB_LEFT, q, left + sib_of, sib).wait_recv()
            gather(SIB_RIGHT, q, right + sib_of, sib).wait_recv()
            gather(SIB_FAR, q, far + sib_of, sib).wait_recv()
            total[...] += jnp.dot(rows[p, k], weights[columns(k), :], preferred_element_type=f32)

            @pl.when(k == chunks - 1)
            def _():
                prefix = table_ref[PREFIX + p]
                angle = frequency_ref[...] * prefix.astype(f32)
                base_cos, base_sin = jnp.cos(angle)[0:1], jnp.sin(angle)[0:1]
                cosine = cos_ref[...] * base_cos - sin_ref[...] * base_sin
                sine = sin_ref[...] * base_cos + cos_ref[...] * base_sin
                lane = lax.broadcasted_iota(jnp.int32, sine.shape, 1)
                sine = jnp.where(lane < HD // 2, -sine, sine)
                for h in range((q_width + kv_width) // HD):
                    place = pl.ds(h * HD, HD)
                    value = total[:, place]
                    value = value * cosine + pltpu.roll(value, HD // 2, axis=1) * sine
                    if h < q_heads:
                        value = value * (HD ** (-0.5) * log2e)
                    packed[p, :, place] = value.astype(bf16)
                place = pl.ds(q_width + kv_width, kv_width)
                packed[p, :, place] = total[:, place].astype(bf16)
                total[...] = jnp.zeros_like(total)

        @pl.when(
            within(tick - attend_near, 0, groups) | within(tick - attend_other, 0, groups)
        )
        def _():
            late = lax.select(tick >= attend_other, 1, 0)
            p = late
            g = tick - attend_near * (1 - late) - attend_other * late
            prefix, span = table_ref[PREFIX + p], table_ref[SPAN + p]
            prefix_rows = cache_k.shape[1]
            keys_new = packed[p, :, pl.ds(q_width, kv_width)]
            values_new = packed[p, :, pl.ds(q_width + kv_width, kv_width)]
            old_column = lax.broadcasted_iota(jnp.int32, (1, prefix_rows), 1)
            old_bias = jnp.where(old_column < prefix, 0.0, masked)
            row = lax.broadcasted_iota(jnp.int32, (span_rows, span_rows), 0)
            column = lax.broadcasted_iota(jnp.int32, (span_rows, span_rows), 1)
            new_bias = jnp.where((column <= row) & (column < span), 0.0, masked)
            def one_head(i, carry):
                h = g * GROUP + i
                query = packed[p, :, head_columns(h)]
                old = lax.dot_general(query, cache_k[p], contract, preferred_element_type=f32)
                old = old + old_bias
                new = lax.dot_general(query, keys_new, contract, preferred_element_type=f32)
                new = new + new_bias
                top = jnp.maximum(
                    jnp.max(old, axis=1, keepdims=True), jnp.max(new, axis=1, keepdims=True)
                )
                old = jnp.exp2(old - top)
                new = jnp.exp2(new - top)
                weight_sum = jnp.sum(old, axis=1, keepdims=True) + jnp.sum(
                    new, axis=1, keepdims=True
                )
                mixed = jnp.dot(old.astype(bf16), cache_v[p], preferred_element_type=f32)
                mixed += jnp.dot(new.astype(bf16), values_new, preferred_element_type=f32)
                heads[p, :, head_columns(h)] = (mixed / weight_sum).astype(bf16)
                return carry

            lax.fori_loop(0, GROUP, one_head, 0)

            @pl.when(p == 0)
            def _():
                near_back(g).start()

            @pl.when(p == 1)
            def _():
                for i in range(len(stage_masks[0])):
                    backs(0, i, g).start()

        for s, lag in enumerate((HEAD_FIRST, HEAD_SECOND)):

            @pl.when(within(tick - attend_other - lag, 0, groups))
            def _(s=s, h=tick - attend_other - lag):
                found = [back_source(s, h)[...]]
                for i in range(len(stage_masks[s])):
                    backs(s, i, h).wait_recv()
                    found.append(back[s, i, h])
                value = mix(found, keep(s))
                if s == 0:
                    backed[h] = value
                    for i in range(len(stage_masks[1])):
                        backs(1, i, h).start()
                else:
                    home[1, :, group_columns(h)] = value

        r, on = reduce_index(tick - RESULT)

        @pl.when(on)
        def _():
            p, j = r // chunks, lax.rem(r, chunks)
            sum_right(r).wait_recv()
            sum_left(r).wait_recv()
            value = (
                kept(r, at(z))[...].astype(f32) + sum_in[r, 0].astype(f32) + sum_in[r, 1].astype(f32)
            ).astype(bf16)

            @pl.when(p == 0)
            def _():
                out_ref[0, :, columns(j)] = value

            @pl.when(p == 1)
            def _():
                first = out_ref[0, :, columns(j)]
                out_ref[0, :, columns(j)] = mix((value, first), flip_flags())
                out_ref[1, :, columns(j)] = mix((first, value), flip_flags())

        return carry

    lax.fori_loop(0, last, tick_body, 0)

    def drain_rows(k, carry):
        near(k).wait_send()
        for s in range(2):
            for i in range(len(stage_masks[s])):
                hops(s, i, k).wait_send()
        return carry

    def drain_sums(q, carry):
        swap(q).wait_send()
        far_sum(q).wait_send()
        sum_right(q).wait_send()
        sum_left(q).wait_send()
        return carry

    def drain_heads(h, carry):
        near_back(h).wait_send()
        for s in range(2):
            for i in range(len(stage_masks[s])):
                backs(s, i, h).wait_send()
        return carry

    lax.fori_loop(0, chunks, drain_rows, 0)
    lax.fori_loop(0, total_chunks, drain_sums, 0)
    lax.fori_loop(0, groups, drain_heads, 0)


def layer(table, x, cosine, sine, frequency, wq, wk, wv, wo, cache_keys, cache_values, chunks=4):
    packets, block, depth = x.shape
    n = lax.axis_size("tensor")
    stage_bits = dp_stage_bits()
    most = max((1 << b) - 1 for b in stage_bits)
    q_width, kv_width = wq.shape[1], wk.shape[1]
    all_width = q_width + 2 * kv_width
    q_heads = q_width // HD
    groups = q_heads // GROUP
    rows, width = block * n, depth // chunks
    bf16, f32 = jnp.bfloat16, jnp.float32
    any_space = pl.BlockSpec(memory_space=pl.ANY)
    smem = pl.BlockSpec(memory_space=pltpu.SMEM)
    vmem = pl.BlockSpec(memory_space=pltpu.VMEM)
    steps = packets * chunks
    dma = pltpu.SemaphoreType.DMA
    return pl.pallas_call(
        functools.partial(layer_kernel, (chunks, stage_bits, q_heads)),
        out_shape=jax.ShapeDtypeStruct((packets, block, depth), bf16),
        in_specs=[smem] + [vmem] * 4 + [any_space] * 6,
        out_specs=vmem,
        scratch_shapes=[
            pltpu.VMEM((packets, chunks, rows, width), bf16),
            pltpu.VMEM((packets, chunks, block, width), bf16),
            pltpu.VMEM((2, most, chunks, block, width), bf16),
            pltpu.VMEM((chunks, block, width), bf16),
            pltpu.VMEM((depth, all_width), bf16),
            pltpu.VMEM((chunks, q_width, width), bf16),
            pltpu.VMEM(cache_keys.shape, bf16),
            pltpu.VMEM(cache_values.shape, bf16),
            pltpu.VMEM((rows, all_width), f32),
            pltpu.VMEM((packets, rows, all_width), bf16),
            pltpu.VMEM((packets, rows, q_width), bf16),
            pltpu.VMEM((2, most, groups, rows, GROUP * HD), bf16),
            pltpu.VMEM((groups, rows, GROUP * HD), bf16),
            pltpu.VMEM((packets, rows, q_width), bf16),
            pltpu.VMEM((steps, rows // 2, width), bf16),
            pltpu.VMEM((steps, block, width), bf16),
            pltpu.VMEM((steps, 2, block, width), bf16),
            dma((5 + chunks,)),
            dma((2, chunks)),
            dma((2, 2, most, chunks)),
            dma((2, 7, steps)),
            dma((2, groups)),
            dma((2, 2, most, groups)),
            dma((2, 4, steps)),
        ],
        compiler_params=pltpu.CompilerParams(
            collective_id=0, has_side_effects=True, vmem_limit_bytes=VMEM_LIMIT
        ),
        name="layer",
    )(table, x, cosine, sine, frequency, wq, wk, wv, wo, cache_keys, cache_values)


def local(
    hidden_rows, norm_gain, w_query, w_key, w_value, w_out, cache_keys, cache_values,
    slot_of_request, span_length, prefix_length,
):
    span_rows = hidden_rows.shape[0] * lax.axis_size("tensor")
    floats = hidden_rows.astype(jnp.float32)
    normed = (
        floats * lax.rsqrt(jnp.mean(floats * floats, axis=-1, keepdims=True) + norm_eps) * norm_gain
    ).astype(jnp.bfloat16)
    half = rope_base ** (-(np.arange(HD // 2, dtype=np.float64) * 2.0 / HD))
    frequency = np.concatenate([half, half])
    angles = np.arange(span_rows, dtype=np.float64)[:, None] * frequency
    result = layer(
        requests_table(slot_of_request, prefix_length, span_length),
        jnp.transpose(normed, (1, 0, 2)),
        jnp.asarray(np.cos(angles), jnp.float32), jnp.asarray(np.sin(angles), jnp.float32),
        jnp.asarray(np.broadcast_to(frequency, (8, HD)), jnp.float32),
        w_query, w_key, w_value, w_out, cache_keys, cache_values,
    )
    return jnp.transpose(result, (1, 0, 2))


def solution(mesh):
    placed = (
        P("tensor", "dp", None),
        P(),
        P(None, "tensor"),
        P(None, "tensor"),
        P(None, "tensor"),
        P("tensor", None),
        P("dp", None, "tensor"),
        P("dp", None, "tensor"),
        P(),
        P(),
        P(),
    )
    return jax.shard_map(
        local, mesh=mesh, in_specs=placed, out_specs=P("tensor", "dp", None), check_vma=False
    )
```

```python
import functools

import jax
import jax.numpy as jnp
import numpy as np
from jax import lax
from jax.experimental import pallas as pl
from jax.experimental.pallas import tpu as pltpu
from jax.sharding import PartitionSpec as P

HD = 128
rope_base = 500000.0
norm_eps = 1e-05
masked = -1e30
log2e = 1.4426950408889634
VMEM_LIMIT = 49 << 20
MESH = pl.DeviceIdType.MESH


def peers():
    n = lax.axis_size("tensor")
    t = lax.axis_index("tensor")
    core = lax.rem(t, 2)
    return t, core, lax.rem(t + 2, n), lax.rem(t + n - 2, n), t + 1 - 2 * core


def greet(devices):
    barrier = pltpu.get_barrier_semaphore()
    for device in devices:
        pl.semaphore_signal(barrier, inc=1, device_id=device, device_id_type=MESH)


def await_greetings(devices):
    pl.semaphore_wait(pltpu.get_barrier_semaphore(), len(devices))


def remote(source, target, sems, index, device):
    return pltpu.make_async_remote_copy(
        src_ref=source,
        dst_ref=target,
        send_sem=sems.at[(0, *index)],
        recv_sem=sems.at[(1, *index)],
        device_id=device,
        device_id_type=MESH,
    )


TO_RIGHT, TO_LEFT, TO_SIB, ONWARD, SIB_LEFT, SIB_RIGHT, SIB_FAR = range(7)
FLIP, SWAPPED, PREFIX, SPAN, KEEP = 0, 1, 2, 4, 6
SWAP, FAR, SUM_RIGHT, SUM_LEFT = range(4)
NEIGHBOURS, FAR_BLOCK, PRODUCT = 2, 4, 5
CHIP_SUM, PASS_ON, RESULT = 1, 3, 5
ROWS_FIRST, ROWS_SECOND = 3, 7
HEAD_FIRST, HEAD_SECOND = 2, 4
GROUP = 1
REDUCE_LAG = 4


def table_kernel(bits, slot_ref, prefix_ref, span_ref, table_ref):
    d = lax.axis_index("dp")
    mask_0 = lax.bitwise_xor(slot_ref[2 * d] // 2, d)
    mask_1 = lax.bitwise_xor(slot_ref[2 * d + 1] // 2, d)
    flip = lax.select(mask_0 != 1, 1, 0)
    mask = mask_0 * flip + mask_1 * (1 - flip)
    table_ref[FLIP] = flip
    low = 1 << bits[1]
    place = KEEP
    for part, count in zip((mask // low, lax.rem(mask, low)), bits):
        for i in range(1 << count):
            table_ref[place] = lax.select(part == i, 1, 0)
            place += 1

    def look_up(i, carry):
        request, prefix_0, prefix_1, span_0, span_1 = carry
        is_0 = lax.select(slot_ref[i] == 2 * d, 1, 0)
        is_1 = lax.select(slot_ref[i] == 2 * d + 1, 1, 0)
        return (
            request + i * is_0,
            prefix_0 + prefix_ref[i] * is_0,
            prefix_1 + prefix_ref[i] * is_1,
            span_0 + span_ref[i] * is_0,
            span_1 + span_ref[i] * is_1,
        )

    request, prefix_0, prefix_1, span_0, span_1 = lax.fori_loop(
        0, slot_ref.shape[0], look_up, (jnp.int32(0),) * 5
    )
    swapped = lax.select(lax.bitwise_xor(request // 2, d) != 1, 1, 0)
    table_ref[SWAPPED] = swapped
    table_ref[PREFIX] = prefix_1 * swapped + prefix_0 * (1 - swapped)
    table_ref[PREFIX + 1] = prefix_0 * swapped + prefix_1 * (1 - swapped)
    table_ref[SPAN] = span_1 * swapped + span_0 * (1 - swapped)
    table_ref[SPAN + 1] = span_0 * swapped + span_1 * (1 - swapped)


def dp_stage_bits():
    bits = lax.axis_size("dp").bit_length() - 1
    return bits - bits // 2, bits // 2


def requests_table(slots, prefix, span):
    bits = dp_stage_bits()
    smem = pl.BlockSpec(memory_space=pltpu.SMEM)
    return pl.pallas_call(
        functools.partial(table_kernel, bits),
        out_shape=jax.ShapeDtypeStruct((KEEP + sum(1 << b for b in bits),), jnp.int32),
        in_specs=[smem] * 3,
        out_specs=smem,
        name="requests_table",
    )(slots, prefix, span)


def layer_kernel(
    plan, table_ref, x_ref, cos_ref, sin_ref, frequency_ref,
    wq_ref, wk_ref, wv_ref, wo_ref, ck_ref, cv_ref, out_ref,
    rows, ordered, hop, hopped, weights, weights_out, cache_k, cache_v, total, packed, heads,
    back, backed, home, swap_in, far_in, sum_in,
    local_sem, near_sem, hop_sem, gather_sem, near_back_sem, back_sem, reduce_sem,
):
    chunks, stage_bits, q_heads = plan
    t, core, right, left, sib = peers()
    n = lax.axis_size("tensor")
    chips = n // 2
    far = lax.rem(t + chips, n)
    z = t // 2
    z_right, z_left, z_far = right // 2, left // 2, far // 2
    d = lax.axis_index("dp")
    block = x_ref.shape[1]
    span_rows = block * n
    width = rows.shape[-1]
    q_width, kv_width = wq_ref.shape[1], wk_ref.shape[1]
    bf16, f32 = jnp.bfloat16, jnp.float32
    total_chunks = 2 * chunks

    def flipped(mask):
        other = d
        for bit in range(mask.bit_length()):
            size = 1 << bit
            if mask & size:
                other = other + size - 2 * size * lax.rem(d // size, 2)
        return {"dp": other}

    def across(device):
        return {"tensor": device}

    stage_masks = (
        [i << stage_bits[1] for i in range(1, 1 << stage_bits[0])],
        list(range(1, 1 << stage_bits[1])),
    )

    def at(device):
        return pl.ds(pl.multiple_of(device * block, block), block)

    def columns(k):
        return pl.ds(pl.multiple_of(k * width, width), width)

    groups = q_heads // GROUP

    def head_columns(h):
        return pl.ds(pl.multiple_of(h * HD, HD), HD)

    def group_columns(g):
        return pl.ds(pl.multiple_of(g * GROUP * HD, GROUP * HD), GROUP * HD)

    def near(k):
        return remote(
            ordered.at[0, k], rows.at[0, k, at(t), :], near_sem, (k,), flipped(1)
        )

    def hop_source(s, k):
        return ordered.at[1, k] if s == 0 else hopped.at[k]

    def hops(s, i, k):
        return remote(
            hop_source(s, k), hop.at[s, i, k], hop_sem, (s, i, k), flipped(stage_masks[s][i])
        )

    def gather(kind, q, owner, device):
        view = rows.at[q // chunks, lax.rem(q, chunks), at(owner), :]
        return remote(view, view, gather_sem, (kind, q), across(device))

    def onward(q):
        odd = lax.rem(q, 2)
        return gather(
            ONWARD, q, left * (1 - odd) + right * odd, right * (1 - odd) + left * odd
        )

    def near_back(h):
        return remote(
            heads.at[0, :, group_columns(h)], home.at[0, :, group_columns(h)],
            near_back_sem, (h,), flipped(1),
        )

    def back_source(s, h):
        return heads.at[1, :, group_columns(h)] if s == 0 else backed.at[h]

    def backs(s, i, h):
        return remote(
            back_source(s, h), back.at[s, i, h], back_sem, (s, i, h), flipped(stage_masks[s][i])
        )

    def kept(r, place):
        return rows.at[r // chunks, lax.rem(r, chunks), place, :]

    def swap(r):
        return remote(
            kept(r, pl.ds(span_rows // 2, span_rows // 2)), swap_in.at[r],
            reduce_sem, (SWAP, r), across(sib),
        )

    def far_sum(r):
        odd = lax.rem(r, 2)
        return remote(
            kept(r, at(z_far)), far_in.at[r], reduce_sem, (FAR, r),
            across(right * (1 - odd) + left * odd),
        )

    def sum_right(r):
        return remote(
            swap_in.at[r, pl.ds(0, block)], sum_in.at[r, 0], reduce_sem, (SUM_RIGHT, r), across(right)
        )

    def sum_left(r):
        return remote(
            swap_in.at[r, pl.ds(block, block)], sum_in.at[r, 1], reduce_sem, (SUM_LEFT, r), across(left)
        )

    def weight_copy(index):
        ref = (wq_ref, wk_ref, wv_ref)[index]
        start = (0, q_width, q_width + kv_width)[index]
        return pltpu.make_async_copy(
            ref, weights.at[:, pl.ds(start, ref.shape[1])], local_sem.at[index]
        )

    def out_copy(j):
        return pltpu.make_async_copy(
            wo_ref.at[:, columns(j)], weights_out.at[j], local_sem.at[5 + j]
        )

    cache_copies = (
        pltpu.make_async_copy(ck_ref, cache_k, local_sem.at[3]),
        pltpu.make_async_copy(cv_ref, cache_v, local_sem.at[4]),
    )

    devices = [across(right), across(left), across(sib)]
    devices += [flipped(m) for masks in stage_masks for m in masks]
    greet(devices)

    def flag(index):
        return table_ref[index].astype(f32)

    def flip_flags():
        return flag(FLIP), 1.0 - flag(FLIP)

    def swap_flags():
        return flag(SWAPPED), 1.0 - flag(SWAPPED)

    def keep(s):
        first = KEEP + s * (1 << stage_bits[0])
        return tuple(flag(first + i) for i in range(1 << stage_bits[s]))

    def mix(parts, flags):
        value = parts[0].astype(f32) * flags[0]
        for part, flag in zip(parts[1:], flags[1:]):
            value = value + part.astype(f32) * flag
        return value.astype(bf16)

    for copy in cache_copies:
        copy.start()

    def order_rows(k, carry):
        first, second = x_ref[0, :, columns(k)], x_ref[1, :, columns(k)]
        ordered[0, k] = mix((second, first), flip_flags())
        ordered[1, k] = mix((first, second), flip_flags())
        return carry

    lax.fori_loop(0, chunks, order_rows, 0)
    total[...] = jnp.zeros_like(total)
    await_greetings(devices)

    def send_rows(k, carry):
        near(k).start()
        for i in range(len(stage_masks[0])):
            hops(0, i, k).start()
        return carry

    lax.fori_loop(0, chunks, send_rows, 0)
    for index in range(3):
        weight_copy(index).start()
    for j in range(chunks):
        out_copy(j).start()

    sib_of = 1 - 2 * core
    attend_near = chunks + PRODUCT
    attend_other = total_chunks + PRODUCT
    reduce_near = attend_near + groups + REDUCE_LAG
    reduce_other = max(attend_other + groups + HEAD_SECOND, reduce_near + chunks)
    last = reduce_other + chunks + RESULT
    contract = (((1,), (1,)), ((), ()))

    def within(value, low, high):
        return (value >= low) & (value < high)

    def reduce_index(tick):
        first = tick - reduce_near
        second = tick - reduce_other
        on_first, on_second = within(first, 0, chunks), within(second, 0, chunks)
        late = lax.select(second >= 0, 1, 0)
        return first * (1 - late) + (second + chunks) * late, on_first | on_second

    def tick_body(tick, carry):
        @pl.when(tick < chunks)
        def _():
            near(tick).wait_recv()

        @pl.when(tick < total_chunks)
        def _():
            gather(TO_RIGHT, tick, t, right).start()
            gather(TO_LEFT, tick, t, left).start()
            gather(TO_SIB, tick, t, sib).start()

        @pl.when(within(tick - NEIGHBOURS, 0, total_chunks))
        def _():
            q = tick - NEIGHBOURS
            gather(TO_RIGHT, q, left, right).wait_recv()
            gather(TO_LEFT, q, right, left).wait_recv()
            onward(q).start()
            gather(SIB_LEFT, q, left, sib).start()
            gather(SIB_RIGHT, q, right, sib).start()

        @pl.when(within(tick - FAR_BLOCK, 0, total_chunks))
        def _():
            q = tick - FAR_BLOCK
            onward(q).wait_recv()
            gather(SIB_FAR, q, far, sib).start()

        for s, lag in enumerate((ROWS_FIRST, ROWS_SECOND)):

            @pl.when(within(tick - lag, 0, chunks))
            def _(s=s, k=tick - lag):
                found = [hop_source(s, k)[...]]
                for i in range(len(stage_masks[s])):
                    hops(s, i, k).wait_recv()
                    found.append(hop[s, i, k])
                value = mix(found, keep(s))
                if s == 0:
                    hopped[k] = value
                    for i in range(len(stage_masks[1])):
                        hops(1, i, k).start()
                else:
                    rows[1, k, at(t), :] = value

        @pl.when(tick == PRODUCT - 1)
        def _():
            for copy in cache_copies:
                copy.wait()
            for cache in (cache_k, cache_v):
                first, second = cache[0], cache[1]
                cache[0] = mix((second, first), swap_flags())
                cache[1] = mix((first, second), swap_flags())
            for index in range(3):
                weight_copy(index).wait()

        r, on = reduce_index(tick - CHIP_SUM)

        @pl.when(on)
        def _():
            swap(r).wait_recv()
            own = kept(r, pl.ds(0, span_rows // 2))
            own[...] = (own[...].astype(f32) + swap_in[r].astype(f32)).astype(bf16)
            far_sum(r).start()

        r, on = reduce_index(tick)

        @pl.when(on)
        def _():
            p, j = r // chunks, lax.rem(r, chunks)

            @pl.when(r == 0)
            def _():
                for g in range(groups):
                    near_back(g).wait_recv()

            @pl.when(r < chunks)
            def _():
                out_copy(j).wait()

            part = jnp.dot(home[p], weights_out[j], preferred_element_type=f32)
            part = part.reshape(chips, 2, block, width)
            gather(TO_RIGHT, r, t, right).wait_send()
            gather(TO_LEFT, r, t, left).wait_send()
            gather(TO_SIB, r, t, sib).wait_send()
            onward(r).wait_send()
            gather(SIB_LEFT, r, left, sib).wait_send()
            gather(SIB_RIGHT, r, right, sib).wait_send()
            gather(SIB_FAR, r, far, sib).wait_send()
            own = jnp.where(core == 0, part[:, 0], part[:, 1]).astype(bf16)
            other = jnp.where(core == 0, part[:, 1], part[:, 0]).astype(bf16)
            kept(r, pl.ds(0, span_rows // 2))[...] = own.reshape(span_rows // 2, width)
            kept(r, pl.ds(span_rows // 2, span_rows // 2))[...] = other.reshape(
                span_rows // 2, width
            )
            swap(r).start()

        @pl.when(within(tick - PRODUCT, 0, total_chunks))
        def _():
            q = tick - PRODUCT
            p, k = q // chunks, lax.rem(q, chunks)
            gather(TO_SIB, q, sib, sib).wait_recv()
            gather(SIB_LEFT, q, left + sib_of, sib).wait_recv()
            gather(SIB_RIGHT, q, right + sib_of, sib).wait_recv()
            gather(SIB_FAR, q, far + sib_of, sib).wait_recv()
            total[...] += jnp.dot(rows[p, k], weights[columns(k), :], preferred_element_type=f32)

            @pl.when(k == chunks - 1)
            def _():
                prefix = table_ref[PREFIX + p]
                angle = frequency_ref[...] * prefix.astype(f32)
                base_cos, base_sin = jnp.cos(angle)[0:1], jnp.sin(angle)[0:1]
                cosine = cos_ref[...] * base_cos - sin_ref[...] * base_sin
                sine = sin_ref[...] * base_cos + cos_ref[...] * base_sin
                lane = lax.broadcasted_iota(jnp.int32, sine.shape, 1)
                sine = jnp.where(lane < HD // 2, -sine, sine)
                for h in range((q_width + kv_width) // HD):
                    place = pl.ds(h * HD, HD)
                    value = total[:, place]
                    value = value * cosine + pltpu.roll(value, HD // 2, axis=1) * sine
                    if h < q_heads:
                        value = value * (HD ** (-0.5) * log2e)
                    packed[p, :, place] = value.astype(bf16)
                place = pl.ds(q_width + kv_width, kv_width)
                packed[p, :, place] = total[:, place].astype(bf16)
                total[...] = jnp.zeros_like(total)

        @pl.when(
            within(tick - attend_near, 0, groups) | within(tick - attend_other, 0, groups)
        )
        def _():
            late = lax.select(tick >= attend_other, 1, 0)
            p = late
            g = tick - attend_near * (1 - late) - attend_other * late
            prefix, span = table_ref[PREFIX + p], table_ref[SPAN + p]
            prefix_rows = cache_k.shape[1]
            keys_new = packed[p, :, pl.ds(q_width, kv_width)]
            values_new = packed[p, :, pl.ds(q_width + kv_width, kv_width)]
            old_column = lax.broadcasted_iota(jnp.int32, (1, prefix_rows), 1)
            old_bias = jnp.where(old_column < prefix, 0.0, masked)
            row = lax.broadcasted_iota(jnp.int32, (span_rows, span_rows), 0)
            column = lax.broadcasted_iota(jnp.int32, (span_rows, span_rows), 1)
            new_bias = jnp.where((column <= row) & (column < span), 0.0, masked)
            def one_head(i, carry):
                h = g * GROUP + i
                query = packed[p, :, head_columns(h)]
                old = lax.dot_general(query, cache_k[p], contract, preferred_element_type=f32)
                old = old + old_bias
                new = lax.dot_general(query, keys_new, contract, preferred_element_type=f32)
                new = new + new_bias
                top = jnp.maximum(
                    jnp.max(old, axis=1, keepdims=True), jnp.max(new, axis=1, keepdims=True)
                )
                old = jnp.exp2(old - top)
                new = jnp.exp2(new - top)
                weight_sum = jnp.sum(old, axis=1, keepdims=True) + jnp.sum(
                    new, axis=1, keepdims=True
                )
                mixed = jnp.dot(old.astype(bf16), cache_v[p], preferred_element_type=f32)
                mixed += jnp.dot(new.astype(bf16), values_new, preferred_element_type=f32)
                heads[p, :, head_columns(h)] = (mixed / weight_sum).astype(bf16)
                return carry

            lax.fori_loop(0, GROUP, one_head, 0)

            @pl.when(p == 0)
            def _():
                near_back(g).start()

            @pl.when(p == 1)
            def _():
                for i in range(len(stage_masks[0])):
                    backs(0, i, g).start()

        for s, lag in enumerate((HEAD_FIRST, HEAD_SECOND)):

            @pl.when(within(tick - attend_other - lag, 0, groups))
            def _(s=s, h=tick - attend_other - lag):
                found = [back_source(s, h)[...]]
                for i in range(len(stage_masks[s])):
                    backs(s, i, h).wait_recv()
                    found.append(back[s, i, h])
                value = mix(found, keep(s))
                if s == 0:
                    backed[h] = value
                    for i in range(len(stage_masks[1])):
                        backs(1, i, h).start()
                else:
                    home[1, :, group_columns(h)] = value

        r, on = reduce_index(tick - PASS_ON)

        @pl.when(on)
        def _():
            odd = lax.rem(r, 2).astype(f32)
            far_sum(r).wait_recv()
            passed = far_in[r].astype(f32)
            swap_in[r, pl.ds(0, block)] = (kept(r, at(z_right))[...].astype(f32) + passed * (1.0 - odd)).astype(bf16)
            swap_in[r, pl.ds(block, block)] = (kept(r, at(z_left))[...].astype(f32) + passed * odd).astype(bf16)
            sum_right(r).start()
            sum_left(r).start()

        r, on = reduce_index(tick - RESULT)

        @pl.when(on)
        def _():
            p, j = r // chunks, lax.rem(r, chunks)
            sum_right(r).wait_recv()
            sum_left(r).wait_recv()
            value = (
                kept(r, at(z))[...].astype(f32) + sum_in[r, 0].astype(f32) + sum_in[r, 1].astype(f32)
            ).astype(bf16)

            @pl.when(p == 0)
            def _():
                out_ref[0, :, columns(j)] = value

            @pl.when(p == 1)
            def _():
                first = out_ref[0, :, columns(j)]
                out_ref[0, :, columns(j)] = mix((value, first), flip_flags())
                out_ref[1, :, columns(j)] = mix((first, value), flip_flags())

        return carry

    lax.fori_loop(0, last, tick_body, 0)

    def drain_rows(k, carry):
        near(k).wait_send()
        for s in range(2):
            for i in range(len(stage_masks[s])):
                hops(s, i, k).wait_send()
        return carry

    def drain_sums(q, carry):
        swap(q).wait_send()
        far_sum(q).wait_send()
        sum_right(q).wait_send()
        sum_left(q).wait_send()
        return carry

    def drain_heads(h, carry):
        near_back(h).wait_send()
        for s in range(2):
            for i in range(len(stage_masks[s])):
                backs(s, i, h).wait_send()
        return carry

    lax.fori_loop(0, chunks, drain_rows, 0)
    lax.fori_loop(0, total_chunks, drain_sums, 0)
    lax.fori_loop(0, groups, drain_heads, 0)


def layer(table, x, cosine, sine, frequency, wq, wk, wv, wo, cache_keys, cache_values, chunks=8):
    packets, block, depth = x.shape
    n = lax.axis_size("tensor")
    stage_bits = dp_stage_bits()
    most = max((1 << b) - 1 for b in stage_bits)
    q_width, kv_width = wq.shape[1], wk.shape[1]
    all_width = q_width + 2 * kv_width
    q_heads = q_width // HD
    groups = q_heads // GROUP
    rows, width = block * n, depth // chunks
    bf16, f32 = jnp.bfloat16, jnp.float32
    any_space = pl.BlockSpec(memory_space=pl.ANY)
    smem = pl.BlockSpec(memory_space=pltpu.SMEM)
    vmem = pl.BlockSpec(memory_space=pltpu.VMEM)
    steps = packets * chunks
    dma = pltpu.SemaphoreType.DMA
    return pl.pallas_call(
        functools.partial(layer_kernel, (chunks, stage_bits, q_heads)),
        out_shape=jax.ShapeDtypeStruct((packets, block, depth), bf16),
        in_specs=[smem] + [vmem] * 4 + [any_space] * 6,
        out_specs=vmem,
        scratch_shapes=[
            pltpu.VMEM((packets, chunks, rows, width), bf16),
            pltpu.VMEM((packets, chunks, block, width), bf16),
            pltpu.VMEM((2, most, chunks, block, width), bf16),
            pltpu.VMEM((chunks, block, width), bf16),
            pltpu.VMEM((depth, all_width), bf16),
            pltpu.VMEM((chunks, q_width, width), bf16),
            pltpu.VMEM(cache_keys.shape, bf16),
            pltpu.VMEM(cache_values.shape, bf16),
            pltpu.VMEM((rows, all_width), f32),
            pltpu.VMEM((packets, rows, all_width), bf16),
            pltpu.VMEM((packets, rows, q_width), bf16),
            pltpu.VMEM((2, most, groups, rows, GROUP * HD), bf16),
            pltpu.VMEM((groups, rows, GROUP * HD), bf16),
            pltpu.VMEM((packets, rows, q_width), bf16),
            pltpu.VMEM((steps, rows // 2, width), bf16),
            pltpu.VMEM((steps, block, width), bf16),
            pltpu.VMEM((steps, 2, block, width), bf16),
            dma((5 + chunks,)),
            dma((2, chunks)),
            dma((2, 2, most, chunks)),
            dma((2, 7, steps)),
            dma((2, groups)),
            dma((2, 2, most, groups)),
            dma((2, 4, steps)),
        ],
        compiler_params=pltpu.CompilerParams(
            collective_id=0, has_side_effects=True, vmem_limit_bytes=VMEM_LIMIT
        ),
        name="layer",
    )(table, x, cosine, sine, frequency, wq, wk, wv, wo, cache_keys, cache_values)


def local(
    hidden_rows, norm_gain, w_query, w_key, w_value, w_out, cache_keys, cache_values,
    slot_of_request, span_length, prefix_length,
):
    span_rows = hidden_rows.shape[0] * lax.axis_size("tensor")
    floats = hidden_rows.astype(jnp.float32)
    normed = (
        floats * lax.rsqrt(jnp.mean(floats * floats, axis=-1, keepdims=True) + norm_eps) * norm_gain
    ).astype(jnp.bfloat16)
    half = rope_base ** (-(np.arange(HD // 2, dtype=np.float64) * 2.0 / HD))
    frequency = np.concatenate([half, half])
    angles = np.arange(span_rows, dtype=np.float64)[:, None] * frequency
    result = layer(
        requests_table(slot_of_request, prefix_length, span_length),
        jnp.transpose(normed, (1, 0, 2)),
        jnp.asarray(np.cos(angles), jnp.float32), jnp.asarray(np.sin(angles), jnp.float32),
        jnp.asarray(np.broadcast_to(frequency, (8, HD)), jnp.float32),
        w_query, w_key, w_value, w_out, cache_keys, cache_values,
    )
    return jnp.transpose(result, (1, 0, 2))


def solution(mesh):
    placed = (
        P("tensor", "dp", None),
        P(),
        P(None, "tensor"),
        P(None, "tensor"),
        P(None, "tensor"),
        P("tensor", None),
        P("dp", None, "tensor"),
        P("dp", None, "tensor"),
        P(),
        P(),
        P(),
    )
    return jax.shard_map(
        local, mesh=mesh, in_specs=placed, out_specs=P("tensor", "dp", None), check_vma=False
    )
```

```python
import functools

import jax
import jax.numpy as jnp
import numpy as np
from jax import lax
from jax.experimental import pallas as pl
from jax.experimental.pallas import tpu as pltpu
from jax.sharding import PartitionSpec as P

HD = 128
rope_base = 500000.0
norm_eps = 1e-05
masked = -1e30
log2e = 1.4426950408889634
VMEM_LIMIT = 49 << 20
MESH = pl.DeviceIdType.MESH


def peers():
    n = lax.axis_size("tensor")
    t = lax.axis_index("tensor")
    core = lax.rem(t, 2)
    return t, core, lax.rem(t + 2, n), lax.rem(t + n - 2, n), t + 1 - 2 * core


def greet(devices):
    barrier = pltpu.get_barrier_semaphore()
    for device in devices:
        pl.semaphore_signal(barrier, inc=1, device_id=device, device_id_type=MESH)


def await_greetings(devices):
    pl.semaphore_wait(pltpu.get_barrier_semaphore(), len(devices))


def remote(source, target, sems, index, device):
    return pltpu.make_async_remote_copy(
        src_ref=source,
        dst_ref=target,
        send_sem=sems.at[(0, *index)],
        recv_sem=sems.at[(1, *index)],
        device_id=device,
        device_id_type=MESH,
    )


TO_RIGHT, TO_LEFT, TO_SIB, ONWARD, SIB_LEFT, SIB_RIGHT, SIB_FAR = range(7)
FLIP, SWAPPED, PREFIX, SPAN, KEEP = 0, 1, 2, 4, 6
SWAP, FAR, SUM_RIGHT, SUM_LEFT = range(4)
NEIGHBOURS, FAR_BLOCK, PRODUCT = 2, 4, 5
CHIP_SUM, PASS_ON, RESULT = 1, 3, 6
ROWS_FIRST, ROWS_SECOND = 3, 7
HEAD_FIRST, HEAD_SECOND = 2, 4
GROUP = 1
REDUCE_LAG = 4


def table_kernel(bits, slot_ref, prefix_ref, span_ref, table_ref):
    d = lax.axis_index("dp")
    mask_0 = lax.bitwise_xor(slot_ref[2 * d] // 2, d)
    mask_1 = lax.bitwise_xor(slot_ref[2 * d + 1] // 2, d)
    flip = lax.select(mask_0 != 1, 1, 0)
    mask = mask_0 * flip + mask_1 * (1 - flip)
    table_ref[FLIP] = flip
    low = 1 << bits[1]
    place = KEEP
    for part, count in zip((mask // low, lax.rem(mask, low)), bits):
        for i in range(1 << count):
            table_ref[place] = lax.select(part == i, 1, 0)
            place += 1

    def look_up(i, carry):
        request, prefix_0, prefix_1, span_0, span_1 = carry
        is_0 = lax.select(slot_ref[i] == 2 * d, 1, 0)
        is_1 = lax.select(slot_ref[i] == 2 * d + 1, 1, 0)
        return (
            request + i * is_0,
            prefix_0 + prefix_ref[i] * is_0,
            prefix_1 + prefix_ref[i] * is_1,
            span_0 + span_ref[i] * is_0,
            span_1 + span_ref[i] * is_1,
        )

    request, prefix_0, prefix_1, span_0, span_1 = lax.fori_loop(
        0, slot_ref.shape[0], look_up, (jnp.int32(0),) * 5
    )
    swapped = lax.select(lax.bitwise_xor(request // 2, d) != 1, 1, 0)
    table_ref[SWAPPED] = swapped
    table_ref[PREFIX] = prefix_1 * swapped + prefix_0 * (1 - swapped)
    table_ref[PREFIX + 1] = prefix_0 * swapped + prefix_1 * (1 - swapped)
    table_ref[SPAN] = span_1 * swapped + span_0 * (1 - swapped)
    table_ref[SPAN + 1] = span_0 * swapped + span_1 * (1 - swapped)


def dp_stage_bits():
    bits = lax.axis_size("dp").bit_length() - 1
    return bits - bits // 2, bits // 2


def requests_table(slots, prefix, span):
    bits = dp_stage_bits()
    smem = pl.BlockSpec(memory_space=pltpu.SMEM)
    return pl.pallas_call(
        functools.partial(table_kernel, bits),
        out_shape=jax.ShapeDtypeStruct((KEEP + sum(1 << b for b in bits),), jnp.int32),
        in_specs=[smem] * 3,
        out_specs=smem,
        name="requests_table",
    )(slots, prefix, span)


def layer_kernel(
    plan, table_ref, x_ref, cos_ref, sin_ref, frequency_ref,
    wq_ref, wk_ref, wv_ref, wo_ref, ck_ref, cv_ref, out_ref,
    rows, ordered, hop, hopped, weights, weights_out, cache_k, cache_v, total, packed, heads,
    back, backed, home, swap_in, far_in, sum_in,
    local_sem, near_sem, hop_sem, gather_sem, near_back_sem, back_sem, reduce_sem,
):
    chunks, stage_bits, q_heads = plan
    t, core, right, left, sib = peers()
    n = lax.axis_size("tensor")
    chips = n // 2
    far = lax.rem(t + chips, n)
    z = t // 2
    z_right, z_left, z_far = right // 2, left // 2, far // 2
    d = lax.axis_index("dp")
    block = x_ref.shape[1]
    span_rows = block * n
    width = rows.shape[-1]
    q_width, kv_width = wq_ref.shape[1], wk_ref.shape[1]
    bf16, f32 = jnp.bfloat16, jnp.float32
    total_chunks = 2 * chunks

    def flipped(mask):
        other = d
        for bit in range(mask.bit_length()):
            size = 1 << bit
            if mask & size:
                other = other + size - 2 * size * lax.rem(d // size, 2)
        return {"dp": other}

    def across(device):
        return {"tensor": device}

    stage_masks = (
        [i << stage_bits[1] for i in range(1, 1 << stage_bits[0])],
        list(range(1, 1 << stage_bits[1])),
    )

    def at(device):
        return pl.ds(pl.multiple_of(device * block, block), block)

    def columns(k):
        return pl.ds(pl.multiple_of(k * width, width), width)

    groups = q_heads // GROUP

    def head_columns(h):
        return pl.ds(pl.multiple_of(h * HD, HD), HD)

    def group_columns(g):
        return pl.ds(pl.multiple_of(g * GROUP * HD, GROUP * HD), GROUP * HD)

    def near(k):
        return remote(
            ordered.at[0, k], rows.at[0, k, at(t), :], near_sem, (k,), flipped(1)
        )

    def hop_source(s, k):
        return ordered.at[1, k] if s == 0 else hopped.at[k]

    def hops(s, i, k):
        return remote(
            hop_source(s, k), hop.at[s, i, k], hop_sem, (s, i, k), flipped(stage_masks[s][i])
        )

    def gather(kind, q, owner, device):
        view = rows.at[q // chunks, lax.rem(q, chunks), at(owner), :]
        return remote(view, view, gather_sem, (kind, q), across(device))

    def onward(q):
        odd = lax.rem(q, 2)
        return gather(
            ONWARD, q, left * (1 - odd) + right * odd, right * (1 - odd) + left * odd
        )

    def near_back(h):
        return remote(
            heads.at[0, :, group_columns(h)], home.at[0, :, group_columns(h)],
            near_back_sem, (h,), flipped(1),
        )

    def back_source(s, h):
        return heads.at[1, :, group_columns(h)] if s == 0 else backed.at[h]

    def backs(s, i, h):
        return remote(
            back_source(s, h), back.at[s, i, h], back_sem, (s, i, h), flipped(stage_masks[s][i])
        )

    def kept(r, place):
        return rows.at[r // chunks, lax.rem(r, chunks), place, :]

    def swap(r):
        return remote(
            kept(r, pl.ds(span_rows // 2, span_rows // 2)), swap_in.at[r],
            reduce_sem, (SWAP, r), across(sib),
        )

    def far_sum(r):
        odd = lax.rem(r, 2)
        return remote(
            kept(r, at(z_far)), far_in.at[r], reduce_sem, (FAR, r),
            across(right * (1 - odd) + left * odd),
        )

    def sum_right(r):
        return remote(
            swap_in.at[r, pl.ds(0, block)], sum_in.at[r, 0], reduce_sem, (SUM_RIGHT, r), across(right)
        )

    def sum_left(r):
        return remote(
            swap_in.at[r, pl.ds(block, block)], sum_in.at[r, 1], reduce_sem, (SUM_LEFT, r), across(left)
        )

    def weight_copy(index):
        ref = (wq_ref, wk_ref, wv_ref)[index]
        start = (0, q_width, q_width + kv_width)[index]
        return pltpu.make_async_copy(
            ref, weights.at[:, pl.ds(start, ref.shape[1])], local_sem.at[index]
        )

    def out_copy(j):
        return pltpu.make_async_copy(
            wo_ref.at[:, columns(j)], weights_out.at[j], local_sem.at[5 + j]
        )

    cache_copies = (
        pltpu.make_async_copy(ck_ref, cache_k, local_sem.at[3]),
        pltpu.make_async_copy(cv_ref, cache_v, local_sem.at[4]),
    )

    devices = [across(right), across(left), across(sib)]
    devices += [flipped(m) for masks in stage_masks for m in masks]
    greet(devices)

    def flag(index):
        return table_ref[index].astype(f32)

    def flip_flags():
        return flag(FLIP), 1.0 - flag(FLIP)

    def swap_flags():
        return flag(SWAPPED), 1.0 - flag(SWAPPED)

    def keep(s):
        first = KEEP + s * (1 << stage_bits[0])
        return tuple(flag(first + i) for i in range(1 << stage_bits[s]))

    def mix(parts, flags):
        value = parts[0].astype(f32) * flags[0]
        for part, flag in zip(parts[1:], flags[1:]):
            value = value + part.astype(f32) * flag
        return value.astype(bf16)

    for copy in cache_copies:
        copy.start()

    def order_rows(k, carry):
        first, second = x_ref[0, :, columns(k)], x_ref[1, :, columns(k)]
        ordered[0, k] = mix((second, first), flip_flags())
        ordered[1, k] = mix((first, second), flip_flags())
        return carry

    lax.fori_loop(0, chunks, order_rows, 0)
    total[...] = jnp.zeros_like(total)
    await_greetings(devices)

    def send_rows(k, carry):
        near(k).start()
        for i in range(len(stage_masks[0])):
            hops(0, i, k).start()
        return carry

    lax.fori_loop(0, chunks, send_rows, 0)
    for index in range(3):
        weight_copy(index).start()
    for j in range(chunks):
        out_copy(j).start()

    sib_of = 1 - 2 * core
    attend_near = chunks + PRODUCT
    attend_other = total_chunks + PRODUCT
    reduce_near = attend_near + groups + REDUCE_LAG
    reduce_other = max(attend_other + groups + HEAD_SECOND, reduce_near + chunks)
    last = reduce_other + chunks + RESULT
    contract = (((1,), (1,)), ((), ()))

    def within(value, low, high):
        return (value >= low) & (value < high)

    def reduce_index(tick):
        first = tick - reduce_near
        second = tick - reduce_other
        on_first, on_second = within(first, 0, chunks), within(second, 0, chunks)
        late = lax.select(second >= 0, 1, 0)
        return first * (1 - late) + (second + chunks) * late, on_first | on_second

    def tick_body(tick, carry):
        @pl.when(tick < chunks)
        def _():
            near(tick).wait_recv()

        @pl.when(tick < total_chunks)
        def _():
            gather(TO_RIGHT, tick, t, right).start()
            gather(TO_LEFT, tick, t, left).start()
            gather(TO_SIB, tick, t, sib).start()

        @pl.when(within(tick - NEIGHBOURS, 0, total_chunks))
        def _():
            q = tick - NEIGHBOURS
            gather(TO_RIGHT, q, left, right).wait_recv()
            gather(TO_LEFT, q, right, left).wait_recv()
            onward(q).start()
            gather(SIB_LEFT, q, left, sib).start()
            gather(SIB_RIGHT, q, right, sib).start()

        @pl.when(within(tick - FAR_BLOCK, 0, total_chunks))
        def _():
            q = tick - FAR_BLOCK
            onward(q).wait_recv()
            gather(SIB_FAR, q, far, sib).start()

        for s, lag in enumerate((ROWS_FIRST, ROWS_SECOND)):

            @pl.when(within(tick - lag, 0, chunks))
            def _(s=s, k=tick - lag):
                found = [hop_source(s, k)[...]]
                for i in range(len(stage_masks[s])):
                    hops(s, i, k).wait_recv()
                    found.append(hop[s, i, k])
                value = mix(found, keep(s))
                if s == 0:
                    hopped[k] = value
                    for i in range(len(stage_masks[1])):
                        hops(1, i, k).start()
                else:
                    rows[1, k, at(t), :] = value

        @pl.when(tick == PRODUCT - 1)
        def _():
            for copy in cache_copies:
                copy.wait()
            for cache in (cache_k, cache_v):
                first, second = cache[0], cache[1]
                cache[0] = mix((second, first), swap_flags())
                cache[1] = mix((first, second), swap_flags())
            for index in range(3):
                weight_copy(index).wait()

        r, on = reduce_index(tick - CHIP_SUM)

        @pl.when(on)
        def _():
            swap(r).wait_recv()
            own = kept(r, pl.ds(0, span_rows // 2))
            own[...] = (own[...].astype(f32) + swap_in[r].astype(f32)).astype(bf16)
            far_sum(r).start()

        r, on = reduce_index(tick)

        @pl.when(on)
        def _():
            p, j = r // chunks, lax.rem(r, chunks)

            @pl.when(r == 0)
            def _():
                for g in range(groups):
                    near_back(g).wait_recv()

            @pl.when(r < chunks)
            def _():
                out_copy(j).wait()

            part = jnp.dot(home[p], weights_out[j], preferred_element_type=f32)
            part = part.reshape(chips, 2, block, width)
            gather(TO_RIGHT, r, t, right).wait_send()
            gather(TO_LEFT, r, t, left).wait_send()
            gather(TO_SIB, r, t, sib).wait_send()
            onward(r).wait_send()
            gather(SIB_LEFT, r, left, sib).wait_send()
            gather(SIB_RIGHT, r, right, sib).wait_send()
            gather(SIB_FAR, r, far, sib).wait_send()
            own = jnp.where(core == 0, part[:, 0], part[:, 1]).astype(bf16)
            other = jnp.where(core == 0, part[:, 1], part[:, 0]).astype(bf16)
            kept(r, pl.ds(0, span_rows // 2))[...] = own.reshape(span_rows // 2, width)
            kept(r, pl.ds(span_rows // 2, span_rows // 2))[...] = other.reshape(
                span_rows // 2, width
            )
            swap(r).start()

        @pl.when(within(tick - PRODUCT, 0, total_chunks))
        def _():
            q = tick - PRODUCT
            p, k = q // chunks, lax.rem(q, chunks)
            gather(TO_SIB, q, sib, sib).wait_recv()
            gather(SIB_LEFT, q, left + sib_of, sib).wait_recv()
            gather(SIB_RIGHT, q, right + sib_of, sib).wait_recv()
            gather(SIB_FAR, q, far + sib_of, sib).wait_recv()
            total[...] += jnp.dot(rows[p, k], weights[columns(k), :], preferred_element_type=f32)

            @pl.when(k == chunks - 1)
            def _():
                prefix = table_ref[PREFIX + p]
                angle = frequency_ref[...] * prefix.astype(f32)
                base_cos, base_sin = jnp.cos(angle)[0:1], jnp.sin(angle)[0:1]
                cosine = cos_ref[...] * base_cos - sin_ref[...] * base_sin
                sine = sin_ref[...] * base_cos + cos_ref[...] * base_sin
                lane = lax.broadcasted_iota(jnp.int32, sine.shape, 1)
                sine = jnp.where(lane < HD // 2, -sine, sine)
                for h in range((q_width + kv_width) // HD):
                    place = pl.ds(h * HD, HD)
                    value = total[:, place]
                    value = value * cosine + pltpu.roll(value, HD // 2, axis=1) * sine
                    if h < q_heads:
                        value = value * (HD ** (-0.5) * log2e)
                    packed[p, :, place] = value.astype(bf16)
                place = pl.ds(q_width + kv_width, kv_width)
                packed[p, :, place] = total[:, place].astype(bf16)
                total[...] = jnp.zeros_like(total)

        @pl.when(
            within(tick - attend_near, 0, groups) | within(tick - attend_other, 0, groups)
        )
        def _():
            late = lax.select(tick >= attend_other, 1, 0)
            p = late
            g = tick - attend_near * (1 - late) - attend_other * late
            prefix, span = table_ref[PREFIX + p], table_ref[SPAN + p]
            prefix_rows = cache_k.shape[1]
            keys_new = packed[p, :, pl.ds(q_width, kv_width)]
            values_new = packed[p, :, pl.ds(q_width + kv_width, kv_width)]
            old_column = lax.broadcasted_iota(jnp.int32, (1, prefix_rows), 1)
            old_bias = jnp.where(old_column < prefix, 0.0, masked)
            row = lax.broadcasted_iota(jnp.int32, (span_rows, span_rows), 0)
            column = lax.broadcasted_iota(jnp.int32, (span_rows, span_rows), 1)
            new_bias = jnp.where((column <= row) & (column < span), 0.0, masked)
            def one_head(i, carry):
                h = g * GROUP + i
                query = packed[p, :, head_columns(h)]
                old = lax.dot_general(query, cache_k[p], contract, preferred_element_type=f32)
                old = old + old_bias
                new = lax.dot_general(query, keys_new, contract, preferred_element_type=f32)
                new = new + new_bias
                top = jnp.maximum(
                    jnp.max(old, axis=1, keepdims=True), jnp.max(new, axis=1, keepdims=True)
                )
                old = jnp.exp2(old - top)
                new = jnp.exp2(new - top)
                weight_sum = jnp.sum(old, axis=1, keepdims=True) + jnp.sum(
                    new, axis=1, keepdims=True
                )
                mixed = jnp.dot(old.astype(bf16), cache_v[p], preferred_element_type=f32)
                mixed += jnp.dot(new.astype(bf16), values_new, preferred_element_type=f32)
                heads[p, :, head_columns(h)] = (mixed / weight_sum).astype(bf16)
                return carry

            lax.fori_loop(0, GROUP, one_head, 0)

            @pl.when(p == 0)
            def _():
                near_back(g).start()

            @pl.when(p == 1)
            def _():
                for i in range(len(stage_masks[0])):
                    backs(0, i, g).start()

        for s, lag in enumerate((HEAD_FIRST, HEAD_SECOND)):

            @pl.when(within(tick - attend_other - lag, 0, groups))
            def _(s=s, h=tick - attend_other - lag):
                found = [back_source(s, h)[...]]
                for i in range(len(stage_masks[s])):
                    backs(s, i, h).wait_recv()
                    found.append(back[s, i, h])
                value = mix(found, keep(s))
                if s == 0:
                    backed[h] = value
                    for i in range(len(stage_masks[1])):
                        backs(1, i, h).start()
                else:
                    home[1, :, group_columns(h)] = value

        r, on = reduce_index(tick - PASS_ON)

        @pl.when(on)
        def _():
            odd = lax.rem(r, 2).astype(f32)
            far_sum(r).wait_recv()
            passed = far_in[r].astype(f32)
            swap_in[r, pl.ds(0, block)] = (kept(r, at(z_right))[...].astype(f32) + passed * (1.0 - odd)).astype(bf16)
            swap_in[r, pl.ds(block, block)] = (kept(r, at(z_left))[...].astype(f32) + passed * odd).astype(bf16)
            sum_right(r).start()
            sum_left(r).start()

        r, on = reduce_index(tick - RESULT)

        @pl.when(on)
        def _():
            p, j = r // chunks, lax.rem(r, chunks)
            sum_right(r).wait_recv()
            sum_left(r).wait_recv()
            value = (
                kept(r, at(z))[...].astype(f32) + sum_in[r, 0].astype(f32) + sum_in[r, 1].astype(f32)
            ).astype(bf16)

            @pl.when(p == 0)
            def _():
                out_ref[0, :, columns(j)] = value

            @pl.when(p == 1)
            def _():
                first = out_ref[0, :, columns(j)]
                out_ref[0, :, columns(j)] = mix((value, first), flip_flags())
                out_ref[1, :, columns(j)] = mix((first, value), flip_flags())

        return carry

    lax.fori_loop(0, last, tick_body, 0)

    def drain_rows(k, carry):
        near(k).wait_send()
        for s in range(2):
            for i in range(len(stage_masks[s])):
                hops(s, i, k).wait_send()
        return carry

    def drain_sums(q, carry):
        swap(q).wait_send()
        far_sum(q).wait_send()
        sum_right(q).wait_send()
        sum_left(q).wait_send()
        return carry

    def drain_heads(h, carry):
        near_back(h).wait_send()
        for s in range(2):
            for i in range(len(stage_masks[s])):
                backs(s, i, h).wait_send()
        return carry

    lax.fori_loop(0, chunks, drain_rows, 0)
    lax.fori_loop(0, total_chunks, drain_sums, 0)
    lax.fori_loop(0, groups, drain_heads, 0)


def layer(table, x, cosine, sine, frequency, wq, wk, wv, wo, cache_keys, cache_values, chunks=8):
    packets, block, depth = x.shape
    n = lax.axis_size("tensor")
    stage_bits = dp_stage_bits()
    most = max((1 << b) - 1 for b in stage_bits)
    q_width, kv_width = wq.shape[1], wk.shape[1]
    all_width = q_width + 2 * kv_width
    q_heads = q_width // HD
    groups = q_heads // GROUP
    rows, width = block * n, depth // chunks
    bf16, f32 = jnp.bfloat16, jnp.float32
    any_space = pl.BlockSpec(memory_space=pl.ANY)
    smem = pl.BlockSpec(memory_space=pltpu.SMEM)
    vmem = pl.BlockSpec(memory_space=pltpu.VMEM)
    steps = packets * chunks
    dma = pltpu.SemaphoreType.DMA
    return pl.pallas_call(
        functools.partial(layer_kernel, (chunks, stage_bits, q_heads)),
        out_shape=jax.ShapeDtypeStruct((packets, block, depth), bf16),
        in_specs=[smem] + [vmem] * 4 + [any_space] * 6,
        out_specs=vmem,
        scratch_shapes=[
            pltpu.VMEM((packets, chunks, rows, width), bf16),
            pltpu.VMEM((packets, chunks, block, width), bf16),
            pltpu.VMEM((2, most, chunks, block, width), bf16),
            pltpu.VMEM((chunks, block, width), bf16),
            pltpu.VMEM((depth, all_width), bf16),
            pltpu.VMEM((chunks, q_width, width), bf16),
            pltpu.VMEM(cache_keys.shape, bf16),
            pltpu.VMEM(cache_values.shape, bf16),
            pltpu.VMEM((rows, all_width), f32),
            pltpu.VMEM((packets, rows, all_width), bf16),
            pltpu.VMEM((packets, rows, q_width), bf16),
            pltpu.VMEM((2, most, groups, rows, GROUP * HD), bf16),
            pltpu.VMEM((groups, rows, GROUP * HD), bf16),
            pltpu.VMEM((packets, rows, q_width), bf16),
            pltpu.VMEM((steps, rows // 2, width), bf16),
            pltpu.VMEM((steps, block, width), bf16),
            pltpu.VMEM((steps, 2, block, width), bf16),
            dma((5 + chunks,)),
            dma((2, chunks)),
            dma((2, 2, most, chunks)),
            dma((2, 7, steps)),
            dma((2, groups)),
            dma((2, 2, most, groups)),
            dma((2, 4, steps)),
        ],
        compiler_params=pltpu.CompilerParams(
            collective_id=0, has_side_effects=True, vmem_limit_bytes=VMEM_LIMIT
        ),
        name="layer",
    )(table, x, cosine, sine, frequency, wq, wk, wv, wo, cache_keys, cache_values)


def local(
    hidden_rows, norm_gain, w_query, w_key, w_value, w_out, cache_keys, cache_values,
    slot_of_request, span_length, prefix_length,
):
    span_rows = hidden_rows.shape[0] * lax.axis_size("tensor")
    floats = hidden_rows.astype(jnp.float32)
    normed = (
        floats * lax.rsqrt(jnp.mean(floats * floats, axis=-1, keepdims=True) + norm_eps) * norm_gain
    ).astype(jnp.bfloat16)
    half = rope_base ** (-(np.arange(HD // 2, dtype=np.float64) * 2.0 / HD))
    frequency = np.concatenate([half, half])
    angles = np.arange(span_rows, dtype=np.float64)[:, None] * frequency
    result = layer(
        requests_table(slot_of_request, prefix_length, span_length),
        jnp.transpose(normed, (1, 0, 2)),
        jnp.asarray(np.cos(angles), jnp.float32), jnp.asarray(np.sin(angles), jnp.float32),
        jnp.asarray(np.broadcast_to(frequency, (8, HD)), jnp.float32),
        w_query, w_key, w_value, w_out, cache_keys, cache_values,
    )
    return jnp.transpose(result, (1, 0, 2))


def solution(mesh):
    placed = (
        P("tensor", "dp", None),
        P(),
        P(None, "tensor"),
        P(None, "tensor"),
        P(None, "tensor"),
        P("tensor", None),
        P("dp", None, "tensor"),
        P("dp", None, "tensor"),
        P(),
        P(),
        P(),
    )
    return jax.shard_map(
        local, mesh=mesh, in_specs=placed, out_specs=P("tensor", "dp", None), check_vma=False
    )
```
